512 devices in a mesh: tm: 16 (over x_lo, z), tile: 32 (over y, x_hi, core).
Axes of the slice: x: 4 (x_hi: 2, x_lo: 2; x = x_hi * 2 + x_lo), y: 8, z: 8, core: 2. Of those that a mesh axis runs over, the one named last changes fastest.
Arguments:
- anomalies: bfloat16 [512, 512, 1440], P('tm', 'tile'), may hold values from -48 to 48
- initial: bfloat16 [16, 512, 1440], P(None, 'tile'), may hold values from -6 to 6
- diffusivity: float32 [512, 1440], P('tile'), may hold values from 0.1 to 1
- land_mask: int32 [512, 1440], P('tile'), may hold values 0 or 1
- threshold: float32 [16], replicated, may hold values from 2 to 8
Outputs:
- loadings: float32 [16, 512, 1440], P(None, 'tile')
- scores: float32 [512, 16], P('tm')
The draws below stay inside these ranges and needn't reach their ends.
All inputs are finite; a program needn't handle non-finite values. No bound on the sum of `land_mask` on one device may be relied on, other than what follows from the above.
Results may differ from the reference program's by a relative error of at most 0.0013.
The reference program's roundings to bfloat16 on the way count: a program that leaves them out, or rounds other values in their place, can miss the bound.
Values sent between devices are 32-bit elements; how exact they have to be, the bound alone decides.
A program may use at most 64 MiB of HBM per device.

```python
import math
import jax
import jax.numpy as jnp
from jax import lax

K = 16
LON = 1440
ITERS = 2
LAT = 512
TIMES = 512


def draw_anomalies(key, part):
    key_noise = jax.random.fold_in(key, 11)
    key_cells = jax.random.fold_in(key, 12)
    key_times = jax.random.fold_in(key, 13)
    cell_scale = jnp.exp(jax.random.uniform(key_cells, (1, LAT, LON), jnp.float32, math.log(0.3), math.log(3.0)))
    time_scale = jnp.exp(jax.random.uniform(key_times, (TIMES, 1, 1), jnp.float32, math.log(0.4), math.log(4.0)))
    noise_part = jnp.clip(jax.random.normal(key_noise, (TIMES, LAT, LON), jnp.float32), -4.0, 4.0)
    values = jnp.clip(noise_part * cell_scale * time_scale, -48.0, 48.0)
    return values.astype(jnp.bfloat16)


def with_ends(values, stream_key, smallest, largest):
    place = [jax.random.randint(jax.random.fold_in(stream_key, axis), (), 0, length) for axis, length in enumerate(values.shape)]
    longest = values.shape.index(max(values.shape))
    beside = place[:longest] + [(place[longest] + 1) % values.shape[longest]] + place[longest + 1:]
    return values.at[tuple(place)].set(smallest).at[tuple(beside)].set(largest)


def block_levels(key, dims, shards, least, top_value):
    level, own = 1.0, jax.random.fold_in(key, 6)
    for position, blocks in shards:
        heights = jnp.exp(jax.random.uniform(jax.random.fold_in(own, position), (blocks,), jnp.float32, least / len(shards), top_value / len(shards)))
        level = level * jnp.repeat(heights, dims[position] // blocks).reshape([-1 if axis == position else 1 for axis in range(len(dims))])
    return level


def noise(own_key, extent, deviation, reach, shards=(), held_as=jnp.bfloat16):
    array = jax.random.normal(own_key, extent, jnp.float32) * deviation
    if len(shards) > 0:
        array = block_levels(own_key, extent, shards, -0.22, 0.18) * array
    return jnp.clip(array, min=-reach, max=reach).astype(held_as)


def setup_inputs(seed: int = 0) -> dict:
    keys = jax.random.split(jax.random.key(seed), 6)
    anomalies = draw_anomalies(jax.random.fold_in(keys[5], 71), 0)
    initial = noise(keys[1], (K, LAT, LON), 1.0, 6.0, ((1, 32),))
    diffusivity = jnp.clip(jnp.exp(math.log(1.0) - 2.3025851 * jax.random.uniform(keys[2], (LAT, LON), jnp.float32) ** block_levels(keys[2], (LAT, LON), ((0, 32),), -0.2, 0.2)), 0.1, 1.0)
    land_mask = with_ends((jax.random.randint(keys[3], (LAT, LON), 0, 10) < 3).astype(jnp.int32), jax.random.fold_in(keys[3], 1), 0, 1)
    threshold = jnp.clip(jax.random.uniform(keys[4], (K,), jnp.float32, 2.0, 8.0), 2.0, 8.0)
    return dict(anomalies=anomalies, initial=initial, diffusivity=diffusivity, land_mask=land_mask, threshold=threshold)


EPS = 1e-06
SHRINK = 0.2

def stencil_weights(diffusivity, land_mask, row_start, lat_total):
    row_index = (row_start + jnp.arange(diffusivity.shape[0], dtype=jnp.int32)).astype(jnp.float32)
    centre = jnp.sin(jnp.pi * (row_index + 0.5) / lat_total)[:, None]
    north_face = jnp.sin(jnp.pi * (row_index + 1.0) / lat_total)[:, None]
    south_face = jnp.sin(jnp.pi * row_index / lat_total)[:, None]
    diffuse = diffusivity * (1.0 + land_mask.astype(jnp.float32)) * 0.5
    return (diffuse, SHRINK * north_face / centre, SHRINK * south_face / centre)

def relax(fields, padded, weights):
    diffuse, north_coef, south_coef = weights
    eastward = jnp.roll(fields, -1, 2)
    westward = jnp.roll(fields, 1, 2)
    upper_row = padded[:, 2:, :]
    lower_row = padded[:, :-2, :]
    change = SHRINK * (eastward + westward - 2.0 * fields) + north_coef * (upper_row - fields) + south_coef * (lower_row - fields)
    return fields + diffuse * change

def smooth(fields, weights):
    for pass_index in range(2):
        padded = jnp.pad(fields, ((0, 0), (1, 1), (0, 0)))
        fields = relax(fields, padded, weights)
    return fields

def prune(values, threshold):
    return jnp.sign(values) * jnp.maximum(jnp.abs(values) - threshold[:, None, None], 0.0)

def reference(anomalies, initial, diffusivity, land_mask, threshold):
    weights = stencil_weights(diffusivity, land_mask, 0, LAT)
    cell_total = LAT * LON
    flattened = anomalies.reshape(TIMES, cell_total)
    current = initial.astype(jnp.float32)
    rounded = initial
    factor = lax.rsqrt(lax.optimization_barrier(jnp.sum(current * current, axis=(1, 2))) / cell_total + EPS)
    scores = jnp.zeros((TIMES, K), jnp.float32)
    for step_index in range(ITERS):
        partial_value = lax.dot_general(flattened, rounded.reshape(K, cell_total), (((1,), (1,)), ((), ())), preferred_element_type=jnp.float32)
        scores = partial_value * factor / math.sqrt(cell_total)
        summed = lax.dot_general(scores.astype(jnp.bfloat16), flattened, (((0,), (0,)), ((), ())), preferred_element_type=jnp.float32)
        current = prune(smooth(summed.reshape(K, LAT, LON), weights), threshold)
        rounded = current.astype(jnp.bfloat16)
        factor = lax.rsqrt(lax.optimization_barrier(jnp.sum(current * current, axis=(1, 2))) / cell_total + EPS)
    return (current * factor[:, None, None], scores)
```

```python
import functools
import math

import jax
import jax.numpy as jnp
from jax import lax
from jax.experimental import pallas as pl
from jax.experimental.pallas import tpu as pltpu
from jax.sharding import PartitionSpec as P

ITERS = 2
EPS = 1e-06
SHRINK = 0.2
MESH = pl.DeviceIdType.MESH
F32 = jnp.float32
BF16 = jnp.bfloat16


def iota(shape, dim):
    return lax.broadcasted_iota(jnp.int32, shape, dim)


def kernel(
    geo,
    anom_hbm,
    init_hbm,
    diff_hbm,
    land_hbm,
    thr_ref,
    cur_out,
    sc_out,
    anom,
    init,
    diff,
    land,
    pa,
    pb,
    ga,
    gb,
    xb,
    xa,
    zr,
    s1,
    s2,
    hs,
    hr,
    ds,
    dr,
    field,
    dcoef,
    ncoef,
    scoef,
    sval,
    load_sem,
    z_s,
    z_r,
    x_s,
    x_r,
    g_s,
    g_r,
    y_s,
    y_r,
    a1_s,
    a1_r,
    a2_s,
    a2_r,
    h_s,
    h_r,
    d_s,
    d_r,
):
    nz, ny, lat_rows, lon, lat_total = geo
    cells = lat_total * lon
    ntile = ny * 4
    tm = lax.axis_index("tm")
    tile = lax.axis_index("tile")
    u = lax.div(tm, nz)
    z = lax.rem(tm, nz)
    v = 1 - u
    core = lax.rem(tile, 2)
    xh = lax.rem(lax.div(tile, 2), 2)
    y = lax.div(tile, 4)
    sg = 1 - 2 * core

    def zat(steps):
        return lax.rem(z + steps * sg + 2 * nz, nz)

    nl = nz // 2
    ns = nl - 1
    plus = {"tm": u * nz + zat(1)}
    minus = {"tm": u * nz + zat(-1)}
    across = {"tm": v * nz + z}
    below = {"tile": lax.rem(tile + ntile - 1, ntile)}
    above = {"tile": lax.rem(tile + 1, ntile)}
    quad = []
    for dx, dc in ((0, 1), (1, 0), (1, 1)):
        px = lax.rem(xh + dx, 2)
        pc = lax.rem(core + dc, 2)
        quad.append((px * 2 + pc, {"tile": y * 4 + px * 2 + pc}))
    column = []
    for dy in range(1, ny):
        to = lax.rem(y + dy, ny)
        frm = lax.rem(y + ny - dy, ny)
        column.append((frm, {"tile": to * 4 + xh * 2 + core}))

    loads = [
        pltpu.make_async_copy(init_hbm, init, load_sem.at[0]),
        pltpu.make_async_copy(anom_hbm, anom, load_sem.at[1]),
        pltpu.make_async_copy(diff_hbm, diff, load_sem.at[2]),
        pltpu.make_async_copy(land_hbm, land, load_sem.at[3]),
    ]
    for copy in loads:
        copy.start()

    barrier = pltpu.get_barrier_semaphore()
    peers = [plus, minus, across, below, above] + [d for _, d in quad] + [d for _, d in column]
    for peer in peers:
        pl.semaphore_signal(barrier, inc=1, device_id=peer, device_id_type=MESH)

    def remote(src, dst, send, recv, where):
        return pltpu.make_async_remote_copy(
            src_ref=src, dst_ref=dst, send_sem=send, recv_sem=recv, device_id=where, device_id_type=MESH
        )

    modes = 2 * nz
    rows = modes * 8
    c_col = iota((rows, 128), 0)
    lane = iota((rows, 128), 1)
    mode_of = lax.rem(lax.div(c_col, 8), 2) * nz + lax.div(c_col, 16)

    loads[2].wait()
    loads[3].wait()
    dcoef[...] = jnp.zeros_like(dcoef)
    diffuse = diff[...] * (1.0 + land[...].astype(F32)) * 0.5
    dcoef[8:24, :lon] = diffuse
    ds[0] = diffuse[0:2]
    ds[1] = diffuse[14:16]
    row_index = (tile * lat_rows + iota((32, 128), 0) - 8).astype(F32)
    centre = jnp.sin(jnp.pi * (row_index + 0.5) / lat_total)
    ncoef[...] = SHRINK * jnp.sin(jnp.pi * (row_index + 1.0) / lat_total) / centre
    scoef[...] = SHRINK * jnp.sin(jnp.pi * row_index / lat_total) / centre

    loads[0].wait()
    for m in range(modes):
        wide = init[m].astype(F32)
        ga[m % nz, m // nz] = wide[0:8]
        gb[m % nz, m // nz] = wide[8:16]
    loads[1].wait()

    pl.semaphore_wait(barrier, len(peers))
    d_copies = [
        remote(ds.at[0], dr.at[1], d_s.at[0], d_r.at[1], below),
        remote(ds.at[1], dr.at[0], d_s.at[1], d_r.at[0], above),
    ]
    for copy in d_copies:
        copy.start()

    def square_row():
        a = ga[...].reshape(rows, lon)
        b = gb[...].reshape(rows, lon)
        total = jnp.sum(a * a + b * b, axis=1, keepdims=True)
        spread = jnp.where((lane >= 64) & (lax.rem(lane, 16) == mode_of), total, 0.0)
        return jnp.sum(spread, axis=0, keepdims=True)

    def over_tile(at, message):
        me = xh * 2 + core
        s1[at, me] = message
        first = [
            remote(s1.at[at, me], s1.at[at, me], a1_s.at[at, j], a1_r.at[at, j], where)
            for j, (_, where) in enumerate(quad)
        ]
        for copy in first:
            copy.start()
        for j, (slot, where) in enumerate(quad):
            remote(s1.at[at, slot], s1.at[at, slot], a1_s.at[at, j], a1_r.at[at, j], where).wait_recv()
        s2[at, y] = (s1[at, 0] + s1[at, 1]) + (s1[at, 2] + s1[at, 3])
        second = [
            remote(s2.at[at, y], s2.at[at, y], a2_s.at[at, j], a2_r.at[at, j], where)
            for j, (_, where) in enumerate(column)
        ]
        for copy in second:
            copy.start()
        for j, (slot, where) in enumerate(column):
            remote(s2.at[at, slot], s2.at[at, slot], a2_s.at[at, j], a2_r.at[at, j], where).wait_recv()
        total = s2[at, 0]
        for j in range(1, ny):
            total = total + s2[at, j]
        for copy in first + second:
            copy.wait_send()
        return total

    def step(it, _):
        half_a = ga[...].reshape(rows, lon)
        half_b = gb[...].reshape(rows, lon)
        rounded = jnp.concatenate([half_a, half_b], axis=0).astype(BF16)
        product = lax.dot_general(anom[...], rounded, (((1,), (1,)), ((), ())), preferred_element_type=F32)
        times = anom.shape[0] // 16
        prod_a = product[:, :rows].reshape(times, 2, 8, rows)
        prod_b = product[:, rows:].reshape(times, 2, 8, rows)
        same = lax.rem(iota((8, rows), 1), 8) == iota((8, rows), 0)
        kept = jnp.where(same, prod_a[:, 0] + prod_b[:, 1], 0.0)
        by_row = jnp.sum(kept, axis=1)
        message = jnp.broadcast_to(square_row(), (8, 128))
        for b in range(4):
            pick = jnp.where(lane == b * 16 + mode_of, 1.0, 0.0).astype(F32)
            message = message + lax.dot_general(
                by_row[b * 8 : (b + 1) * 8],
                pick,
                (((1,), (0,)), ((), ())),
                precision=lax.Precision.HIGHEST,
                preferred_element_type=F32,
            )
        total = over_tile(it, message)
        factor = lax.rsqrt(pltpu.roll(total, 64, 1) / cells + EPS)
        scores = total * factor / math.sqrt(cells)
        scores = jnp.where(iota((8, 128), 1) < 64, scores, 0.0)
        sval[...] = scores

        tall = jnp.broadcast_to(scores.reshape(8, 1, 128), (8, 16, 128)).reshape(128, 128)
        tall = tall.T.astype(BF16)
        left = []
        for b in range(4):
            pick = jnp.where(lane == b * 16 + mode_of, 1.0, 0.0).astype(BF16)
            wide = jnp.dot(pick, tall, preferred_element_type=F32)
            at_a = lax.rem(lane, 16) == lax.rem(c_col, 8)
            at_b = lax.rem(lane, 16) == lax.rem(c_col, 8) + 8
            left.append(jnp.concatenate([jnp.where(at_a, wide, 0.0), jnp.where(at_b, wide, 0.0)], axis=0).astype(BF16))
        spread = jnp.concatenate(left, axis=1)
        part = jnp.dot(spread, anom[...], preferred_element_type=F32)
        pb[...] = part[rows:].reshape(nz, 2, 8, lon)
        pa[...] = part[:rows].reshape(nz, 2, 8, lon)

        sent = []

        def go(copy):
            copy.start()
            sent.append(copy)

        offsets = [nl]
        for r in range(ns, 0, -1):
            offsets += [-r, r]
        offsets += [0]
        place = {off: q for q, off in enumerate(offsets)}
        x_in = [remote(pb.at[zat(off), v], xb.at[q], x_s.at[q], x_r.at[q], across) for q, off in enumerate(offsets)]

        def own(c, off):
            if c == 0:
                return pa.at[zat(off), v]
            if c == 1:
                return pa.at[zat(off), u]
            return xb.at[place[off]]

        def prepare(off):
            q = place[off]
            x_in[q].wait_recv()
            xb[q] = xb[q] + pb[zat(off), u]

        def z_copy(c, r, long):
            slot = r if long else nl + r
            top = nl if long else ns
            if r == top - 1:
                src = own(c, top if long else -top)
            else:
                src = zr.at[c, slot + 1]
            return remote(src, zr.at[c, slot], z_s.at[c, slot], z_r.at[c, slot], plus if long else minus)

        for copy in x_in:
            go(copy)
        for c in (0, 1):
            go(z_copy(c, nl - 1, True))
            go(z_copy(c, ns - 1, False))
        prepare(nl)
        go(z_copy(2, nl - 1, True))
        prepare(-ns)
        go(z_copy(2, ns - 1, False))
        for r in range(nl - 1, 0, -1):
            for c in (0, 1, 2):
                if c == 2:
                    prepare(r)
                z_copy(c, r, True).wait_recv()
                zr[c, r] = zr[c, r] + own(c, r)[...]
                go(z_copy(c, r - 1, True))
                q = r - 1
                if q > 0:
                    if c == 2:
                        prepare(-q)
                    z_copy(c, q, False).wait_recv()
                    zr[c, nl + q] = zr[c, nl + q] + own(c, -q)[...]
                    go(z_copy(c, q - 1, False))
        prepare(0)

        def last(c):
            z_copy(c, 0, False).wait_recv()
            z_copy(c, 0, True).wait_recv()
            return own(c, 0)[...] + zr[c, 0] + zr[c, nl]

        xa[0] = last(0)
        x_last = remote(xa.at[0], xa.at[1], x_s.at[nz], x_r.at[nz], across)
        go(x_last)
        mine = last(1)
        sum_b = last(2)
        hs[1] = sum_b[6:8]
        h_up = remote(hs.at[1], hr.at[0], h_s.at[1], h_r.at[0], above)
        go(h_up)
        x_last.wait_recv()
        sum_a = mine + xa[1]
        hs[0] = sum_a[0:2]
        h_down = remote(hs.at[0], hr.at[1], h_s.at[0], h_r.at[1], below)
        go(h_down)

        width = field.shape[1]
        col = iota((32, width), 1)

        def wrapped(values):
            right = pltpu.roll(values, lon, 1)
            left = pltpu.roll(values, width - lon, 1)
            return jnp.where(col < lon, values, jnp.where(col < (lon + width) // 2, right, left))

        @pl.when(it == 0)
        def _():
            for copy in d_copies:
                copy.wait_recv()
            dcoef[6:8, :lon] = dr[0]
            dcoef[24:26, :lon] = dr[1]
            dcoef[...] = wrapped(dcoef[...])

        field[8:16, :lon] = sum_a
        field[16:24, :lon] = sum_b
        h_up.wait_recv()
        h_down.wait_recv()
        field[6:8, :lon] = hr[0]
        field[24:26, :lon] = hr[1]
        local_row = iota((32, width), 0) - 8
        global_row = local_row + tile * lat_rows
        inside = (global_row >= 0) & (global_row < lat_total) & (local_row >= -2) & (local_row < 18)
        f = jnp.where(inside, wrapped(field[...]), 0.0)
        north = ncoef[:, 0:1]
        south = scoef[:, 0:1]
        for _pass in range(2):
            east = pltpu.roll(f, width - 1, 1)
            west = pltpu.roll(f, 1, 1)
            upper = pltpu.roll(f, 31, 0)
            lower = pltpu.roll(f, 1, 0)
            change = SHRINK * (east + west - 2.0 * f) + north * (upper - f) + south * (lower - f)
            f = jnp.where(inside, f + dcoef[...] * change, 0.0)
        smoothed = f[8:24, :lon]
        shrunk = jnp.maximum(jnp.abs(smoothed) - thr_ref[tm], 0.0)
        pruned = jnp.where(smoothed < 0.0, -shrunk, shrunk)
        ga[z, u] = pruned[0:8]
        gb[z, u] = pruned[8:16]

        def g_ref(c, off):
            if c == 0:
                return ga.at[zat(off), u]
            if c == 1:
                return gb.at[zat(off), u]
            return ga.at[zat(off), v]

        def g_copy(c, h, long):
            ref = g_ref(c, 1 - h if long else h - 1)
            slot = h - 1 if long else nl + h - 1
            return remote(ref, ref, g_s.at[c, slot], g_r.at[c, slot], plus if long else minus)

        def g_wait(c, h, long):
            ref = g_ref(c, -h if long else h)
            slot = h - 1 if long else nl + h - 1
            remote(ref, ref, g_s.at[c, slot], g_r.at[c, slot], plus if long else minus).wait_recv()

        def y_copy(q, off):
            ref = gb.at[zat(off), u]
            return remote(ref, ref, y_s.at[q], y_r.at[q], across)

        while sent:
            sent.pop().wait_send()
        a_mine = ga.at[z, u]
        go(remote(a_mine, a_mine, y_s.at[nz], y_r.at[nz], across))
        for c in (0, 1):
            go(g_copy(c, 1, True))
            go(g_copy(c, 1, False))
        go(y_copy(0, 0))
        a_other = ga.at[z, v]
        remote(a_other, a_other, y_s.at[nz], y_r.at[nz], across).wait_recv()
        go(g_copy(2, 1, True))
        go(g_copy(2, 1, False))
        queue = [0]
        for h in range(1, nl + 1):
            for c in (0, 1, 2):
                g_wait(c, h, True)
                if h < nl:
                    go(g_copy(c, h + 1, True))
                if c == 1:
                    go(y_copy(len(queue), -h))
                    queue.append(-h)
                if h <= ns:
                    g_wait(c, h, False)
                    if h < ns:
                        go(g_copy(c, h + 1, False))
                    if c == 1:
                        go(y_copy(len(queue), h))
                        queue.append(h)
        for q, off in enumerate(queue):
            ref = gb.at[zat(off), v]
            remote(ref, ref, y_s.at[q], y_r.at[q], across).wait_recv()
        for copy in sent:
            copy.wait_send()
        return 0

    lax.fori_loop(0, ITERS, step, 0)
    for copy in d_copies:
        copy.wait_send()

    total = over_tile(ITERS, jnp.broadcast_to(square_row(), (8, 128)))
    factor = lax.rsqrt(total / cells + EPS)
    picked = jnp.where(lane == 64 + mode_of, jnp.broadcast_to(factor[0:1], (rows, 128)), 0.0)
    column_factor = jnp.sum(picked, axis=1, keepdims=True)
    out_a = ga[...].reshape(rows, lon) * column_factor
    out_b = gb[...].reshape(rows, lon) * column_factor
    for m in range(modes):
        c = (m % nz) * 16 + (m // nz) * 8
        cur_out[m, 0:8] = out_a[c : c + 8]
        cur_out[m, 8:16] = out_b[c : c + 8]
    for b in range(4):
        moved = sval[...] if b == 0 else pltpu.roll(sval[...], 128 - 16 * b, 1)
        sc_out[b * 8 : (b + 1) * 8, :] = moved[:, :16]


def solution(mesh):
    nz = mesh.shape["tm"] // 2
    ny = mesh.shape["tile"] // 4

    def local(anomalies, initial, diffusivity, land_mask, threshold):
        times, lat_rows, lon = anomalies.shape
        modes = initial.shape[0]
        lat_total = lat_rows * mesh.shape["tile"]
        width = (lon + 127) // 128 * 128
        vmem = pltpu.VMEM
        dma = pltpu.SemaphoreType.DMA
        any_space = pl.BlockSpec(memory_space=pl.ANY)
        in_vmem = pl.BlockSpec(memory_space=pltpu.VMEM)
        half = (nz, 2, 8, lon)
        return pl.pallas_call(
            functools.partial(kernel, (nz, ny, lat_rows, lon, lat_total)),
            out_shape=(
                jax.ShapeDtypeStruct((modes, lat_rows, lon), F32),
                jax.ShapeDtypeStruct((times, modes), F32),
            ),
            in_specs=[any_space] * 4 + [pl.BlockSpec(memory_space=pltpu.SMEM)],
            out_specs=(in_vmem, in_vmem),
            scratch_shapes=[
                vmem((times * lat_rows, lon), BF16),
                vmem((modes, lat_rows, lon), BF16),
                vmem((lat_rows, lon), F32),
                vmem((lat_rows, lon), jnp.int32),
                vmem(half, F32),
                vmem(half, F32),
                vmem(half, F32),
                vmem(half, F32),
                vmem((nz, 8, lon), F32),
                vmem((2, 8, lon), F32),
                vmem((3, nz - 1, 8, lon), F32),
                vmem((ITERS + 1, 4, 8, 128), F32),
                vmem((ITERS + 1, ny, 8, 128), F32),
                vmem((2, 2, lon), F32),
                vmem((2, 2, lon), F32),
                vmem((2, 2, lon), F32),
                vmem((2, 2, lon), F32),
                vmem((32, width), F32),
                vmem((32, width), F32),
                vmem((32, 128), F32),
                vmem((32, 128), F32),
                vmem((8, 128), F32),
                dma((4,)),
                dma((3, nz - 1)),
                dma((3, nz - 1)),
                dma((nz + 1,)),
                dma((nz + 1,)),
                dma((3, nz - 1)),
                dma((3, nz - 1)),
                dma((nz + 1,)),
                dma((nz + 1,)),
                dma((ITERS + 1, 3)),
                dma((ITERS + 1, 3)),
                dma((ITERS + 1, ny - 1)),
                dma((ITERS + 1, ny - 1)),
                dma((2,)),
                dma((2,)),
                dma((2,)),
                dma((2,)),
            ],
            compiler_params=pltpu.CompilerParams(
                collective_id=0, has_side_effects=True, vmem_limit_bytes=48 * 1024 * 1024
            ),
        )(anomalies.reshape(times * lat_rows, lon), initial, diffusivity, land_mask, threshold)

    return jax.shard_map(
        local,
        mesh=mesh,
        in_specs=(
            P("tm", "tile", None),
            P(None, "tile", None),
            P("tile", None),
            P("tile", None),
            P(),
        ),
        out_specs=(P(None, "tile", None), P("tm", None)),
        check_vma=False,
    )
```

```python
import functools
import math

import jax
import jax.numpy as jnp
from jax import lax
from jax.experimental import pallas as pl
from jax.experimental.pallas import tpu as pltpu
from jax.sharding import PartitionSpec as P

ITERS = 2
EPS = 1e-06
SHRINK = 0.2
MESH = pl.DeviceIdType.MESH
F32 = jnp.float32
BF16 = jnp.bfloat16


def iota(shape, dim):
    return lax.broadcasted_iota(jnp.int32, shape, dim)


def kernel(
    geo,
    anom_hbm,
    init_hbm,
    diff_hbm,
    land_hbm,
    thr_hbm,
    cur_out,
    sc_out,
    anom,
    init,
    diff,
    land,
    thr_ref,
    pa,
    pb,
    ga,
    gb,
    xb,
    xa,
    zr,
    s1,
    s2,
    fr,
    hs,
    hr,
    ds,
    dr,
    field,
    dcoef,
    ncoef,
    scoef,
    sval,
    fac,
    msg,
    load_sem,
    z_s,
    z_r,
    x_s,
    x_r,
    g_s,
    g_r,
    y_s,
    y_r,
    a1_s,
    a1_r,
    a2_s,
    a2_r,
    f_s,
    f_r,
    h_s,
    h_r,
    d_s,
    d_r,
):
    nz, ny, lat_rows, lon, lat_total = geo
    cells = lat_total * lon
    ntile = ny * 4
    tm = lax.axis_index("tm")
    tile = lax.axis_index("tile")
    u = lax.div(tm, nz)
    z = lax.rem(tm, nz)
    v = 1 - u
    core = lax.rem(tile, 2)
    xh = lax.rem(lax.div(tile, 2), 2)
    y = lax.div(tile, 4)
    sg = 1 - 2 * core

    def zat(steps):
        return lax.rem(z + steps * sg + 2 * nz, nz)

    plus = {"tm": u * nz + zat(1)}
    plus2 = {"tm": u * nz + zat(2)}
    minus = {"tm": u * nz + zat(-1)}
    minus2 = {"tm": u * nz + zat(-2)}
    across = {"tm": v * nz + z}
    below = {"tile": lax.rem(tile + ntile - 1, ntile)}
    above = {"tile": lax.rem(tile + 1, ntile)}
    mate = {"tile": tile + sg}
    spread_to = []
    for dy in sorted(range(ny), key=lambda d: -min(d, ny - d)):
        for dx in (1, 0):
            if dy or dx:
                ox = lax.rem(xh + dx, 2)
                to = lax.rem(y + dy, ny)
                frm = lax.rem(y + ny - dy, ny)
                spread_to.append((frm * 2 + ox, {"tile": to * 4 + ox * 2 + core}))
    factor_to = []
    for dz in sorted(range(nz), key=lambda d: -min(d, nz - d)):
        for du in (1, 0):
            if dz or du:
                ou = lax.rem(u + du, 2)
                to = lax.rem(z + dz, nz)
                frm = lax.rem(z + nz - dz, nz)
                factor_to.append((ou * nz + frm, {"tm": ou * nz + to}))

    loads = [
        pltpu.make_async_copy(init_hbm, init, load_sem.at[0]),
        pltpu.make_async_copy(anom_hbm, anom, load_sem.at[1]),
        pltpu.make_async_copy(diff_hbm, diff, load_sem.at[2]),
        pltpu.make_async_copy(land_hbm, land, load_sem.at[3]),
        pltpu.make_async_copy(thr_hbm, thr_ref, load_sem.at[4]),
    ]
    for copy in loads:
        copy.start()

    barrier = pltpu.get_barrier_semaphore()
    peers = [below, above, mate] + [d for _, d in spread_to] + [d for _, d in factor_to]
    for peer in peers:
        pl.semaphore_signal(barrier, inc=1, device_id=peer, device_id_type=MESH)

    def remote(src, dst, send, recv, where):
        return pltpu.make_async_remote_copy(
            src_ref=src, dst_ref=dst, send_sem=send, recv_sem=recv, device_id=where, device_id_type=MESH
        )

    modes = 2 * nz
    rows = modes * 8
    c_col = iota((rows, 128), 0)
    lane = iota((rows, 128), 1)
    mode_of = lax.rem(lax.div(c_col, 8), 2) * nz + lax.div(c_col, 16)

    def row_in_band(i):
        return i + 4, jnp.where(i < 4, i, i + 8)

    loads[2].wait()
    loads[3].wait()
    dcoef[...] = jnp.zeros_like(dcoef)
    diffuse = diff[...] * (1.0 + land[...].astype(F32)) * 0.5
    dcoef[8:24, :lon] = diffuse
    ds[0] = diffuse[0:2]
    ds[1] = diffuse[14:16]
    row_index = (tile * lat_rows + iota((32, 128), 0) - 8).astype(F32)
    centre = jnp.sin(jnp.pi * (row_index + 0.5) / lat_total)
    ncoef[...] = SHRINK * jnp.sin(jnp.pi * (row_index + 1.0) / lat_total) / centre
    scoef[...] = SHRINK * jnp.sin(jnp.pi * row_index / lat_total) / centre

    loads[0].wait()
    for m in range(modes):
        wide = init[m].astype(F32)
        ga[m % nz, m // nz] = wide[4:12]
        gb[m % nz, m // nz] = jnp.concatenate([wide[0:4], wide[12:16]], axis=0)
    loads[1].wait()
    loads[4].wait()

    def square_row():
        a = ga[...].reshape(rows, lon)
        b = gb[...].reshape(rows, lon)
        total = jnp.sum(a * a + b * b, axis=1, keepdims=True)
        spread = jnp.where((lane >= 64) & (lax.rem(lane, 16) == mode_of), total, 0.0)
        return jnp.sum(spread, axis=0, keepdims=True)

    def partial_scores():
        half_a = ga[...].reshape(rows, lon)
        half_b = gb[...].reshape(rows, lon)
        rounded = jnp.concatenate([half_a, half_b], axis=0).astype(BF16)
        product = lax.dot_general(anom[...], rounded, (((1,), (1,)), ((), ())), preferred_element_type=F32)
        times = anom.shape[0] // 16
        prod_a = product[:, :rows].reshape(times, 16, rows)
        prod_b = product[:, rows:].reshape(times, 16, rows)
        here = iota((16, rows), 0)
        in_a, in_b = row_in_band(lax.rem(iota((16, rows), 1), 8))
        kept = jnp.where(here == in_a, prod_a, 0.0) + jnp.where(here == in_b, prod_b, 0.0)
        by_row = jnp.sum(kept, axis=1)
        message = jnp.zeros((8, 128), F32)
        for b in range(4):
            pick = jnp.where(lane == b * 16 + mode_of, 1.0, 0.0).astype(F32)
            message = message + lax.dot_general(
                by_row[b * 8 : (b + 1) * 8],
                pick,
                (((1,), (0,)), ((), ())),
                precision=lax.Precision.HIGHEST,
                preferred_element_type=F32,
            )
        return message

    msg[...] = partial_scores() + square_row()

    pl.semaphore_wait(barrier, len(peers))
    d_copies = [
        remote(ds.at[0], dr.at[1], d_s.at[0], d_r.at[1], below),
        remote(ds.at[1], dr.at[0], d_s.at[1], d_r.at[0], above),
    ]
    for copy in d_copies:
        copy.start()

    def step(it, _):
        late = []

        def go(copy, waits):
            copy.start()
            waits.append(copy)

        def tile_first(at, message):
            s1[at, core] = message
            go(remote(s1.at[at, core], s1.at[at, core], a1_s.at[at], a1_r.at[at], mate), late)

        def tile_second(at):
            other = s1.at[at, 1 - core]
            remote(other, other, a1_s.at[at], a1_r.at[at], mate).wait_recv()
            me = y * 2 + xh
            s2[at, me] = s1[at, 0] + s1[at, 1]
            for j, (_, where) in enumerate(spread_to):
                go(remote(s2.at[at, me], s2.at[at, me], a2_s.at[at, j], a2_r.at[at, j], where), late)

        def tile_total(at):
            for j, (slot, where) in enumerate(spread_to):
                remote(s2.at[at, slot], s2.at[at, slot], a2_s.at[at, j], a2_r.at[at, j], where).wait_recv()
            return jnp.sum(s2[at], axis=0)

        tile_first(it, msg[...])
        tile_second(it)
        total = tile_total(it)

        @pl.when(it == 0)
        def _():
            fac[...] = lax.rsqrt(pltpu.roll(total, 64, 1) / cells + EPS)

        scores = total * fac[...] / math.sqrt(cells)
        scores = jnp.where(iota((8, 128), 1) < 64, scores, 0.0)
        sval[...] = scores

        tall = jnp.broadcast_to(scores.reshape(8, 1, 128), (8, 16, 128)).reshape(128, 128)
        tall = tall.T.astype(BF16)
        left = []
        for b in range(4):
            pick = jnp.where(lane == b * 16 + mode_of, 1.0, 0.0).astype(BF16)
            wide = jnp.dot(pick, tall, preferred_element_type=F32)
            in_a, in_b = row_in_band(lax.rem(c_col, 8))
            here = lax.rem(lane, 16)
            left.append(
                jnp.concatenate([jnp.where(here == in_a, wide, 0.0), jnp.where(here == in_b, wide, 0.0)], axis=0).astype(BF16)
            )
        spread = jnp.concatenate(left, axis=1)
        part = jnp.dot(spread, anom[...], preferred_element_type=F32)
        pb[...] = part[rows:].reshape(nz, 2, 8, lon)
        pa[...] = part[:rows].reshape(nz, 2, 8, lon)

        early = []
        offsets = (4, 3, -3, 2, -2, 1, -1, 0)
        place = {off: q for q, off in enumerate(offsets)}
        x_in = [remote(pb.at[zat(off), v], xb.at[q], x_s.at[q], x_r.at[q], across) for q, off in enumerate(offsets)]
        slots = {4: 0, 3: 1, 2: 2, 1: 3, -3: 4, -2: 5, -1: 6}

        def own(c, off):
            if c == 0:
                return pa.at[zat(off), v]
            if c == 1:
                return pa.at[zat(off), u]
            return xb.at[place[off]]

        def prepare(c, off):
            if c == 2:
                q = place[off]
                x_in[q].wait_recv()
                xb[q] = xb[q] + pb[zat(off), u]

        def z_copy(c, off):
            slot = slots[off]
            if off in (4, 3, -3):
                src = own(c, off)
            else:
                src = zr.at[c, {2: 0, 1: 2, -2: 4, -1: 5}[off]]
            where = plus2 if off == 4 else plus if off > 0 else minus
            return remote(src, zr.at[c, slot], z_s.at[c, slot], z_r.at[c, slot], where)

        for copy in x_in[:3]:
            go(copy, late)
        for c in (0, 1):
            for off in (4, 3, -3):
                go(z_copy(c, off), early)
        for copy in x_in[3:]:
            go(copy, late)
        for off in (4, 3, -3):
            prepare(2, off)
            go(z_copy(2, off), early)
        for c in (0, 1, 2):
            prepare(c, 2)
            z_copy(c, 3).wait_recv()
            z_copy(c, 4).wait_recv()
            zr[c, 0] = zr[c, 0] + zr[c, 1] + own(c, 2)[...]
            go(z_copy(c, 2), early)
            prepare(c, -2)
            z_copy(c, -3).wait_recv()
            zr[c, 4] = zr[c, 4] + own(c, -2)[...]
            go(z_copy(c, -2), early)
        for c in (0, 1, 2):
            prepare(c, 1)
            z_copy(c, 2).wait_recv()
            zr[c, 2] = zr[c, 2] + own(c, 1)[...]
            go(z_copy(c, 1), early)
            prepare(c, -1)
            z_copy(c, -2).wait_recv()
            zr[c, 5] = zr[c, 5] + own(c, -1)[...]
            go(z_copy(c, -1), early)
        prepare(2, 0)

        def last(c):
            z_copy(c, 1).wait_recv()
            z_copy(c, -1).wait_recv()
            return own(c, 0)[...] + zr[c, 3] + zr[c, 6]

        xa[0] = last(0)
        x_last = remote(xa.at[0], xa.at[1], x_s.at[nz], x_r.at[nz], across)
        go(x_last, late)
        mine = last(1)
        sum_b = last(2)
        hs[0] = sum_b[0:2]
        hs[1] = sum_b[6:8]
        h_up = remote(hs.at[1], hr.at[0], h_s.at[1], h_r.at[0], above)
        h_down = remote(hs.at[0], hr.at[1], h_s.at[0], h_r.at[1], below)
        go(h_up, late)
        go(h_down, late)

        width = field.shape[1]
        col = iota((32, width), 1)

        def wrapped(values):
            right = pltpu.roll(values, lon, 1)
            left = pltpu.roll(values, width - lon, 1)
            return jnp.where(col < lon, values, jnp.where(col < (lon + width) // 2, right, left))

        @pl.when(it == 0)
        def _():
            for copy in d_copies:
                copy.wait_recv()
            dcoef[6:8, :lon] = dr[0]
            dcoef[24:26, :lon] = dr[1]
            dcoef[...] = wrapped(dcoef[...])

        field[8:12, :lon] = sum_b[0:4]
        field[20:24, :lon] = sum_b[4:8]
        for copy in early:
            copy.wait_send()
        x_last.wait_recv()
        field[12:20, :lon] = mine + xa[1]
        h_up.wait_recv()
        h_down.wait_recv()
        field[6:8, :lon] = hr[0]
        field[24:26, :lon] = hr[1]
        local_row = iota((32, width), 0) - 8
        global_row = local_row + tile * lat_rows
        inside = (global_row >= 0) & (global_row < lat_total) & (local_row >= -2) & (local_row < 18)
        f = jnp.where(inside, wrapped(field[...]), 0.0)
        north = ncoef[:, 0:1]
        south = scoef[:, 0:1]
        for _pass in range(2):
            east = pltpu.roll(f, width - 1, 1)
            west = pltpu.roll(f, 1, 1)
            upper = pltpu.roll(f, 31, 0)
            lower = pltpu.roll(f, 1, 0)
            change = SHRINK * (east + west - 2.0 * f) + north * (upper - f) + south * (lower - f)
            f = jnp.where(inside, f + dcoef[...] * change, 0.0)
        smoothed = f[8:24, :lon]
        shrunk = jnp.maximum(jnp.abs(smoothed) - thr_ref[tm], 0.0)
        pruned = jnp.where(smoothed < 0.0, -shrunk, shrunk)
        ga[z, u] = pruned[4:12]
        gb[z, u] = jnp.concatenate([pruned[0:4], pruned[12:16]], axis=0)

        def g_ref(c, off):
            if c == 0:
                return ga.at[zat(off), u]
            if c == 1:
                return gb.at[zat(off), u]
            return ga.at[zat(off), v]

        def g_copy(c, off):
            from_here = {1: 0, 2: 0, 3: -2, 4: -3, -1: 0, -2: 1, -3: 2}[off]
            ref = g_ref(c, from_here)
            where = plus2 if off == 2 else plus if off > 0 else minus
            return remote(ref, ref, g_s.at[c, slots_g[off]], g_r.at[c, slots_g[off]], where)

        def g_wait(c, off):
            ref = g_ref(c, -off)
            remote(ref, ref, g_s.at[c, slots_g[off]], g_r.at[c, slots_g[off]], plus).wait_recv()

        slots_g = {1: 0, 2: 1, 3: 2, 4: 3, -1: 4, -2: 5, -3: 6}
        queue = []

        def y_send(off):
            ref = gb.at[zat(off), u]
            q = len(queue)
            queue.append(off)
            go(remote(ref, ref, y_s.at[q], y_r.at[q], across), late)

        a_mine = ga.at[z, u]
        go(remote(a_mine, a_mine, y_s.at[nz], y_r.at[nz], across), late)
        for c in (0, 1):
            for off in (2, -1, 1):
                go(g_copy(c, off), late)
        y_send(0)
        squares = jnp.sum(jnp.sum(pruned * pruned, axis=1, keepdims=True), axis=0, keepdims=True)
        tile_first(ITERS + it, jnp.broadcast_to(squares, (8, 128)))
        tile_second(ITERS + it)
        a_other = ga.at[z, v]
        remote(a_other, a_other, y_s.at[nz], y_r.at[nz], across).wait_recv()
        for off in (2, -1, 1):
            go(g_copy(2, off), late)
        for c in (0, 1, 2):
            g_wait(c, 2)
            go(g_copy(c, 3), late)
            g_wait(c, -1)
            go(g_copy(c, -2), late)
            g_wait(c, 1)
            if c == 1:
                for off in (-2, 1, -1):
                    y_send(off)
        here = tile_total(ITERS + it)
        fr[it, tm] = lax.rsqrt(here / cells + EPS)
        for j, (_, where) in enumerate(factor_to):
            go(remote(fr.at[it, tm], fr.at[it, tm], f_s.at[it, j], f_r.at[it, j], where), late)
        for c in (0, 1, 2):
            g_wait(c, 3)
            go(g_copy(c, 4), late)
            g_wait(c, -2)
            go(g_copy(c, -3), late)
            if c == 1:
                for off in (-3, 2):
                    y_send(off)
        for c in (1, 0, 2):
            g_wait(c, 4)
            g_wait(c, -3)
            if c == 1:
                for off in (-4, 3):
                    y_send(off)
        for j, (slot, where) in enumerate(factor_to):
            remote(fr.at[it, slot], fr.at[it, slot], f_s.at[it, j], f_r.at[it, j], where).wait_recv()
        every = fr[it][:, 0, :]
        every = jnp.where(lax.rem(iota((modes, 128), 1), 16) == iota((modes, 128), 0), every, 0.0)
        fac[...] = jnp.broadcast_to(jnp.sum(every, axis=0, keepdims=True), (8, 128))
        for q, off in enumerate(queue):
            ref = gb.at[zat(off), v]
            remote(ref, ref, y_s.at[q], y_r.at[q], across).wait_recv()

        @pl.when(it + 1 < ITERS)
        def _():
            msg[...] = partial_scores()

        for copy in late:
            copy.wait_send()
        return 0

    lax.fori_loop(0, ITERS, step, 0)

    picked = jnp.where(lane == mode_of, jnp.broadcast_to(fac[0:1], (rows, 128)), 0.0)
    column_factor = jnp.sum(picked, axis=1, keepdims=True)
    out_a = ga[...].reshape(rows, lon) * column_factor
    out_b = gb[...].reshape(rows, lon) * column_factor
    for m in range(modes):
        c = (m % nz) * 16 + (m // nz) * 8
        cur_out[m, 4:12] = out_a[c : c + 8]
        cur_out[m, 0:4] = out_b[c : c + 4]
        cur_out[m, 12:16] = out_b[c + 4 : c + 8]
    for b in range(4):
        moved = sval[...] if b == 0 else pltpu.roll(sval[...], 128 - 16 * b, 1)
        sc_out[b * 8 : (b + 1) * 8, :] = moved[:, :16]
    for copy in d_copies:
        copy.wait_send()


def solution(mesh):
    nz = mesh.shape["tm"] // 2
    ny = mesh.shape["tile"] // 4

    def local(anomalies, initial, diffusivity, land_mask, threshold):
        times, lat_rows, lon = anomalies.shape
        modes = initial.shape[0]
        lat_total = lat_rows * mesh.shape["tile"]
        width = (lon + 127) // 128 * 128
        vmem = pltpu.VMEM
        dma = pltpu.SemaphoreType.DMA
        in_hbm = pl.BlockSpec(memory_space=pltpu.HBM)
        in_vmem = pl.BlockSpec(memory_space=pltpu.VMEM)
        half = (nz, 2, 8, lon)
        return pl.pallas_call(
            functools.partial(kernel, (nz, ny, lat_rows, lon, lat_total)),
            out_shape=(
                jax.ShapeDtypeStruct((modes, lat_rows, lon), F32),
                jax.ShapeDtypeStruct((times, modes), F32),
            ),
            in_specs=[in_hbm] * 5,
            out_specs=(in_vmem, in_vmem),
            scratch_shapes=[
                vmem((times * lat_rows, lon), BF16),
                vmem((modes, lat_rows, lon), BF16),
                vmem((lat_rows, lon), F32),
                vmem((lat_rows, lon), jnp.int32),
                pltpu.SMEM((modes,), F32),
                vmem(half, F32),
                vmem(half, F32),
                vmem(half, F32),
                vmem(half, F32),
                vmem((nz, 8, lon), F32),
                vmem((2, 8, lon), F32),
                vmem((3, nz - 1, 8, lon), F32),
                vmem((2 * ITERS, 2, 8, 128), F32),
                vmem((2 * ITERS, 2 * ny, 8, 128), F32),
                vmem((ITERS, modes, 8, 128), F32),
                vmem((2, 2, lon), F32),
                vmem((2, 2, lon), F32),
                vmem((2, 2, lon), F32),
                vmem((2, 2, lon), F32),
                vmem((32, width), F32),
                vmem((32, width), F32),
                vmem((32, 128), F32),
                vmem((32, 128), F32),
                vmem((8, 128), F32),
                vmem((8, 128), F32),
                vmem((8, 128), F32),
                dma((5,)),
                dma((3, nz - 1)),
                dma((3, nz - 1)),
                dma((nz + 1,)),
                dma((nz + 1,)),
                dma((3, nz - 1)),
                dma((3, nz - 1)),
                dma((nz + 1,)),
                dma((nz + 1,)),
                dma((2 * ITERS,)),
                dma((2 * ITERS,)),
                dma((2 * ITERS, 2 * ny - 1)),
                dma((2 * ITERS, 2 * ny - 1)),
                dma((ITERS, modes - 1)),
                dma((ITERS, modes - 1)),
                dma((2,)),
                dma((2,)),
                dma((2,)),
                dma((2,)),
            ],
            compiler_params=pltpu.CompilerParams(
                collective_id=0, has_side_effects=True, vmem_limit_bytes=60 * 1024 * 1024
            ),
        )(anomalies.reshape(times * lat_rows, lon), initial, diffusivity, land_mask, threshold)

    return jax.shard_map(
        local,
        mesh=mesh,
        in_specs=(
            P("tm", "tile", None),
            P(None, "tile", None),
            P("tile", None),
            P("tile", None),
            P(),
        ),
        out_specs=(P(None, "tile", None), P("tm", None)),
        check_vma=False,
    )
```

```python
import functools
import math

import jax
import jax.numpy as jnp
from jax import lax
from jax.experimental import pallas as pl
from jax.experimental.pallas import tpu as pltpu
from jax.sharding import PartitionSpec as P

ITERS = 2
EPS = 1e-06
SHRINK = 0.2
MESH = pl.DeviceIdType.MESH
F32 = jnp.float32
BF16 = jnp.bfloat16


def iota(shape, dim):
    return lax.broadcasted_iota(jnp.int32, shape, dim)


def kernel(
    geo,
    anom_hbm,
    init_hbm,
    diff_hbm,
    land_hbm,
    thr_hbm,
    ga_out,
    gb_out,
    fac_out,
    score_out,
    anom,
    init,
    diff,
    land,
    thr_ref,
    pa,
    pb,
    ga,
    gb,
    xb,
    xa,
    zr,
    s1,
    s2,
    fr,
    hs,
    hr,
    ds,
    dr,
    field,
    dcoef,
    ncoef,
    scoef,
    sval,
    fac,
    msg,
    load_sem,
    z_s,
    z_r,
    x_s,
    x_r,
    g_s,
    g_r,
    y_s,
    y_r,
    a1_s,
    a1_r,
    a2_s,
    a2_r,
    f_s,
    f_r,
    h_s,
    h_r,
    d_s,
    d_r,
):
    nz, ny, lat_rows, lon, lat_total = geo
    cells = lat_total * lon
    ntile = ny * 4
    tm = lax.axis_index("tm")
    tile = lax.axis_index("tile")
    u = lax.div(tm, nz)
    z = lax.rem(tm, nz)
    v = 1 - u
    core = lax.rem(tile, 2)
    xh = lax.rem(lax.div(tile, 2), 2)
    y = lax.div(tile, 4)
    sg = 1 - 2 * core

    def zat(steps):
        return lax.rem(z + steps * sg + 2 * nz, nz)

    plus = {"tm": u * nz + zat(1)}
    plus2 = {"tm": u * nz + zat(2)}
    minus = {"tm": u * nz + zat(-1)}
    across = {"tm": v * nz + z}
    plus_across = {"tm": v * nz + zat(1)}
    plus2_across = {"tm": v * nz + zat(2)}
    minus_across = {"tm": v * nz + zat(-1)}
    below = {"tile": lax.rem(tile + ntile - 1, ntile)}
    above = {"tile": lax.rem(tile + 1, ntile)}
    mate = {"tile": tile + sg}
    spread_to = []
    for dy in sorted(range(ny), key=lambda d: -min(d, ny - d)):
        for dx in (1, 0):
            if dy or dx:
                ox = lax.rem(xh + dx, 2)
                to = lax.rem(y + dy, ny)
                frm = lax.rem(y + ny - dy, ny)
                spread_to.append((frm * 2 + ox, {"tile": to * 4 + ox * 2 + core}))
    factor_to = []
    for dz in sorted(range(nz), key=lambda d: -min(d, nz - d)):
        for du in (1, 0):
            if dz or du:
                ou = lax.rem(u + du, 2)
                to = lax.rem(z + dz, nz)
                frm = lax.rem(z + nz - dz, nz)
                factor_to.append((ou * nz + frm, {"tm": ou * nz + to}))

    loads = [
        pltpu.make_async_copy(init_hbm, init, load_sem.at[0]),
        pltpu.make_async_copy(anom_hbm, anom, load_sem.at[1]),
        pltpu.make_async_copy(diff_hbm, diff, load_sem.at[2]),
        pltpu.make_async_copy(land_hbm, land, load_sem.at[3]),
        pltpu.make_async_copy(thr_hbm, thr_ref, load_sem.at[4]),
    ]
    for copy in loads:
        copy.start()

    barrier = pltpu.get_barrier_semaphore()
    peers = [below, above, mate] + [d for _, d in spread_to] + [d for _, d in factor_to]
    for peer in peers:
        pl.semaphore_signal(barrier, inc=1, device_id=peer, device_id_type=MESH)

    def remote(src, dst, send, recv, where):
        return pltpu.make_async_remote_copy(
            src_ref=src, dst_ref=dst, send_sem=send, recv_sem=recv, device_id=where, device_id_type=MESH
        )

    modes = 2 * nz
    rows = modes * 8
    c_col = iota((rows, 128), 0)
    lane = iota((rows, 128), 1)
    mode_of = lax.rem(lax.div(c_col, 8), 2) * nz + lax.div(c_col, 16)

    def row_in_band(i):
        return jnp.where(i < 4, i, i + 8), i + 4

    loads[0].wait()
    for m in range(modes):
        wide = init[m].astype(F32)
        ga[m % nz, m // nz] = jnp.concatenate([wide[0:4], wide[12:16]], axis=0)
        gb[m % nz, m // nz] = wide[4:12]
    loads[1].wait()

    def square_row():
        a = ga[...].reshape(rows, lon)
        b = gb[...].reshape(rows, lon)
        total = jnp.sum(a * a + b * b, axis=1, keepdims=True)
        spread = jnp.where((lane >= 64) & (lax.rem(lane, 16) == mode_of), total, 0.0)
        return jnp.sum(spread, axis=0, keepdims=True)

    def partial_scores():
        half_a = ga[...].reshape(rows, lon)
        half_b = gb[...].reshape(rows, lon)
        rounded = jnp.concatenate([half_a, half_b], axis=0).astype(BF16)
        product = lax.dot_general(anom[...], rounded, (((1,), (1,)), ((), ())), preferred_element_type=F32)
        times = anom.shape[0] // 16
        prod_a = product[:, :rows].reshape(times, 16, rows)
        prod_b = product[:, rows:].reshape(times, 16, rows)
        here = iota((16, rows), 0)
        in_a, in_b = row_in_band(lax.rem(iota((16, rows), 1), 8))
        kept = jnp.where(here == in_a, prod_a, 0.0) + jnp.where(here == in_b, prod_b, 0.0)
        by_row = jnp.sum(kept, axis=1)
        message = jnp.zeros((8, 128), F32)
        for b in range(4):
            pick = jnp.where(lane == b * 16 + mode_of, 1.0, 0.0).astype(F32)
            message = message + lax.dot_general(
                by_row[b * 8 : (b + 1) * 8],
                pick,
                (((1,), (0,)), ((), ())),
                precision=lax.Precision.HIGHEST,
                preferred_element_type=F32,
            )
        return message

    msg[...] = partial_scores() + square_row()

    pl.semaphore_wait(barrier, len(peers))
    d_copies = [
        remote(ds.at[0], dr.at[1], d_s.at[0], d_r.at[1], below),
        remote(ds.at[1], dr.at[0], d_s.at[1], d_r.at[0], above),
    ]

    def coefficients():
        loads[2].wait()
        loads[3].wait()
        dcoef[...] = jnp.zeros_like(dcoef)
        diffuse = diff[...] * (1.0 + land[...].astype(F32)) * 0.5
        dcoef[8:24, :lon] = diffuse
        ds[0] = diffuse[0:2]
        ds[1] = diffuse[14:16]
        row_index = (tile * lat_rows + iota((32, 128), 0) - 8).astype(F32)
        centre = jnp.sin(jnp.pi * (row_index + 0.5) / lat_total)
        ncoef[...] = SHRINK * jnp.sin(jnp.pi * (row_index + 1.0) / lat_total) / centre
        scoef[...] = SHRINK * jnp.sin(jnp.pi * row_index / lat_total) / centre
        for copy in d_copies:
            copy.start()
        loads[4].wait()

    def step(it, _):
        late = []

        def go(copy, waits):
            copy.start()
            waits.append(copy)

        def tile_first(at, message):
            s1[at, core] = message
            go(remote(s1.at[at, core], s1.at[at, core], a1_s.at[at], a1_r.at[at], mate), late)

        def tile_second(at):
            other = s1.at[at, 1 - core]
            remote(other, other, a1_s.at[at], a1_r.at[at], mate).wait_recv()
            me = y * 2 + xh
            s2[at, me] = s1[at, 0] + s1[at, 1]
            for j, (_, where) in enumerate(spread_to):
                go(remote(s2.at[at, me], s2.at[at, me], a2_s.at[at, j], a2_r.at[at, j], where), late)

        def tile_total(at):
            for j, (slot, where) in enumerate(spread_to):
                remote(s2.at[at, slot], s2.at[at, slot], a2_s.at[at, j], a2_r.at[at, j], where).wait_recv()
            return jnp.sum(s2[at], axis=0)

        tile_first(it, msg[...])
        tile_second(it)
        pl.when(it == 0)(coefficients)
        total = tile_total(it)

        @pl.when(it == 0)
        def _():
            fac[...] = lax.rsqrt(pltpu.roll(total, 64, 1) / cells + EPS)

        scores = total * fac[...] / math.sqrt(cells)
        scores = jnp.where(iota((8, 128), 1) < 64, scores, 0.0)
        sval[...] = scores

        tall = jnp.broadcast_to(scores.reshape(8, 1, 128), (8, 16, 128)).reshape(128, 128)
        tall = tall.T.astype(BF16)
        left = []
        for b in range(4):
            pick = jnp.where(lane == b * 16 + mode_of, 1.0, 0.0).astype(BF16)
            wide = jnp.dot(pick, tall, preferred_element_type=F32)
            in_a, in_b = row_in_band(lax.rem(c_col, 8))
            here = lax.rem(lane, 16)
            left.append(
                jnp.concatenate([jnp.where(here == in_a, wide, 0.0), jnp.where(here == in_b, wide, 0.0)], axis=0).astype(BF16)
            )
        spread = jnp.concatenate(left, axis=1)
        part = jnp.dot(spread, anom[...], preferred_element_type=F32)
        pb[...] = part[rows:].reshape(nz, 2, 8, lon)
        pa[...] = part[:rows].reshape(nz, 2, 8, lon)

        early = []
        offsets = (4, 3, -3, 2, -2, 1, -1, 0)
        place = {off: q for q, off in enumerate(offsets)}
        x_in = [remote(pb.at[zat(off), v], xb.at[q], x_s.at[q], x_r.at[q], across) for q, off in enumerate(offsets)]
        slots = {4: 0, 3: 1, 2: 2, 1: 3, -3: 4, -2: 5, -1: 6}

        def own(c, off):
            if c == 0:
                return pa.at[zat(off), v]
            if c == 1:
                return pa.at[zat(off), u]
            return xb.at[place[off]]

        def prepare(c, off):
            if c == 2:
                q = place[off]
                x_in[q].wait_recv()
                xb[q] = xb[q] + pb[zat(off), u]

        def z_copy(c, off):
            slot = slots[off]
            if off in (4, 3, -3):
                src = own(c, off)
            else:
                src = zr.at[c, {2: 0, 1: 2, -2: 4, -1: 5}[off]]
            where = plus2 if off == 4 else plus if off > 0 else minus
            if c == 0 and off in (1, -1):
                where = plus_across if off > 0 else minus_across
            return remote(src, zr.at[c, slot], z_s.at[c, slot], z_r.at[c, slot], where)

        for copy in x_in[:3]:
            go(copy, late)
        x_own = remote(pa.at[z, v], xa, x_s.at[nz], x_r.at[nz], across)
        for c in (0, 1):
            for off in (4, 3, -3):
                go(z_copy(c, off), early)
        for copy in x_in[3:] + [x_own]:
            go(copy, late)
        for off in (4, 3, -3):
            prepare(2, off)
            go(z_copy(2, off), early)
        for c in (0, 1, 2):
            prepare(c, 2)
            z_copy(c, 3).wait_recv()
            z_copy(c, 4).wait_recv()
            zr[c, 0] = zr[c, 0] + zr[c, 1] + own(c, 2)[...]
            go(z_copy(c, 2), early)
            prepare(c, -2)
            z_copy(c, -3).wait_recv()
            zr[c, 4] = zr[c, 4] + own(c, -2)[...]
            go(z_copy(c, -2), early)
        for c in (0, 1, 2):
            prepare(c, 1)
            z_copy(c, 2).wait_recv()
            zr[c, 2] = zr[c, 2] + own(c, 1)[...]
            go(z_copy(c, 1), early)
            prepare(c, -1)
            z_copy(c, -2).wait_recv()
            zr[c, 5] = zr[c, 5] + own(c, -1)[...]
            go(z_copy(c, -1), early)
        def last(c):
            z_copy(c, 1).wait_recv()
            z_copy(c, -1).wait_recv()
            return zr[c, 3] + zr[c, 6]

        x_own.wait_recv()
        sum_a = (pa[z, u] + xa[...]) + last(0) + last(1)
        hs[0] = sum_a[0:2]
        hs[1] = sum_a[6:8]
        h_up = remote(hs.at[1], hr.at[0], h_s.at[1], h_r.at[0], above)
        h_down = remote(hs.at[0], hr.at[1], h_s.at[0], h_r.at[1], below)
        go(h_up, late)
        go(h_down, late)
        prepare(2, 0)
        sum_b = xb[place[0]] + last(2)

        width = field.shape[1]
        col = iota((32, width), 1)

        def wrapped(values):
            right = pltpu.roll(values, lon, 1)
            left = pltpu.roll(values, width - lon, 1)
            return jnp.where(col < lon, values, jnp.where(col < (lon + width) // 2, right, left))

        @pl.when(it == 0)
        def _():
            for copy in d_copies:
                copy.wait_recv()
            dcoef[6:8, :lon] = dr[0]
            dcoef[24:26, :lon] = dr[1]
            dcoef[...] = wrapped(dcoef[...])

        field[8:12, :lon] = sum_a[0:4]
        field[20:24, :lon] = sum_a[4:8]
        field[12:20, :lon] = sum_b
        for copy in early:
            copy.wait_send()
        h_up.wait_recv()
        h_down.wait_recv()
        field[6:8, :lon] = hr[0]
        field[24:26, :lon] = hr[1]
        local_row = iota((32, width), 0) - 8
        global_row = local_row + tile * lat_rows
        inside = (global_row >= 0) & (global_row < lat_total) & (local_row >= -2) & (local_row < 18)
        f = jnp.where(inside, wrapped(field[...]), 0.0)
        north = ncoef[:, 0:1]
        south = scoef[:, 0:1]
        for _pass in range(2):
            east = pltpu.roll(f, width - 1, 1)
            west = pltpu.roll(f, 1, 1)
            upper = pltpu.roll(f, 31, 0)
            lower = pltpu.roll(f, 1, 0)
            change = SHRINK * (east + west - 2.0 * f) + north * (upper - f) + south * (lower - f)
            f = jnp.where(inside, f + dcoef[...] * change, 0.0)
        smoothed = f[8:24, :lon]
        shrunk = jnp.maximum(jnp.abs(smoothed) - thr_ref[tm], 0.0)
        pruned = jnp.where(smoothed < 0.0, -shrunk, shrunk)
        ga[z, u] = jnp.concatenate([pruned[0:4], pruned[12:16]], axis=0)
        gb[z, u] = pruned[4:12]

        def g_ref(c, off):
            if c == 0:
                return ga.at[zat(off), u]
            if c == 1:
                return gb.at[zat(off), u]
            return ga.at[zat(off), v]

        def g_copy(c, off):
            from_here = {1: 0, 2: 0, 3: -2, 4: -3, -1: 0, -2: 1, -3: 2}[off]
            ref = g_ref(c, from_here)
            where = plus2 if off == 2 else plus if off > 0 else minus
            if c == 2 and off in (1, 2, -1):
                ref = ga.at[z, u]
                where = {1: plus_across, 2: plus2_across, -1: minus_across}[off]
            return remote(ref, ref, g_s.at[c, slots_g[off]], g_r.at[c, slots_g[off]], where)

        def g_wait(c, off):
            ref = g_ref(c, -off)
            remote(ref, ref, g_s.at[c, slots_g[off]], g_r.at[c, slots_g[off]], plus).wait_recv()

        slots_g = {1: 0, 2: 1, 3: 2, 4: 3, -1: 4, -2: 5, -3: 6}
        queue = []

        def y_send(off, ahead=0):
            ref = gb.at[zat(off), u]
            q = len(queue)
            queue.append(off - ahead)
            where = {0: across, 1: plus_across, -1: minus_across}[ahead]
            go(remote(ref, ref, y_s.at[q], y_r.at[q], where), late)

        for off in (2, -1, 1):
            for c in (0, 2, 1):
                go(g_copy(c, off), late)
        a_mine = ga.at[z, u]
        go(remote(a_mine, a_mine, y_s.at[nz], y_r.at[nz], across), late)
        y_send(0)
        squares = jnp.sum(jnp.sum(pruned * pruned, axis=1, keepdims=True), axis=0, keepdims=True)
        tile_first(ITERS + it, jnp.broadcast_to(squares, (8, 128)))
        tile_second(ITERS + it)
        for c in (1, 0, 2):
            g_wait(c, 2)
            go(g_copy(c, 3), late)
            g_wait(c, -1)
            go(g_copy(c, -2), late)
            g_wait(c, 1)
            if c == 1:
                for off in (-2, 1, -1):
                    y_send(off)
        here = tile_total(ITERS + it)
        fr[it, tm] = lax.rsqrt(here / cells + EPS)
        for j, (_, where) in enumerate(factor_to):
            go(remote(fr.at[it, tm], fr.at[it, tm], f_s.at[it, j], f_r.at[it, j], where), late)
        for c in (1, 0, 2):
            g_wait(c, 3)
            go(g_copy(c, 4), late)
            if c == 1:
                y_send(-3, 1)
            g_wait(c, -2)
            go(g_copy(c, -3), late)
            if c == 1:
                y_send(2, -1)
                y_send(-3)
                y_send(2)
        a_other = ga.at[z, v]
        remote(a_other, a_other, y_s.at[nz], y_r.at[nz], across).wait_recv()
        for c in (1, 0, 2):
            g_wait(c, 4)
            g_wait(c, -3)
        for j, (slot, where) in enumerate(factor_to):
            remote(fr.at[it, slot], fr.at[it, slot], f_s.at[it, j], f_r.at[it, j], where).wait_recv()
        every = fr[it][:, 0, :]
        every = jnp.where(lax.rem(iota((modes, 128), 1), 16) == iota((modes, 128), 0), every, 0.0)
        fac[...] = jnp.broadcast_to(jnp.sum(every, axis=0, keepdims=True), (8, 128))
        for q, off in enumerate(queue):
            ref = gb.at[zat(off), v]
            remote(ref, ref, y_s.at[q], y_r.at[q], across).wait_recv()

        @pl.when(it + 1 < ITERS)
        def _():
            msg[...] = partial_scores()

        for copy in late:
            copy.wait_send()
        return 0

    lax.fori_loop(0, ITERS, step, 0)

    stores = [
        pltpu.make_async_copy(ga, ga_out, load_sem.at[0]),
        pltpu.make_async_copy(gb, gb_out, load_sem.at[1]),
    ]
    for copy in stores:
        copy.start()
    fac_out[...] = fac[...]
    score_out[...] = sval[...]
    for copy in d_copies:
        copy.wait_send()
    for copy in stores:
        copy.wait()


def finish(nz, ga, gb, fac, sval, cur_out, score_out):
    at = pl.program_id(0) * 2
    lane = iota((1, 128), 1)
    for b in range(2):
        for u in range(2):
            factor = jnp.sum(jnp.where(lane == u * nz + at + b, fac[0:1], 0.0), axis=1, keepdims=True)
            half_a = ga[b, u] * factor
            cur_out[u, b, 0:4] = half_a[0:4]
            cur_out[u, b, 4:12] = gb[b, u] * factor
            cur_out[u, b, 12:16] = half_a[4:8]
    turned = sval[...].T
    for b in range(4):
        score_out[:, b * 8 : (b + 1) * 8] = turned[b * 16 : (b + 1) * 16]


def solution(mesh):
    nz = mesh.shape["tm"] // 2
    ny = mesh.shape["tile"] // 4

    def local(anomalies, initial, diffusivity, land_mask, threshold):
        times, lat_rows, lon = anomalies.shape
        modes = initial.shape[0]
        lat_total = lat_rows * mesh.shape["tile"]
        width = (lon + 127) // 128 * 128
        vmem = pltpu.VMEM
        dma = pltpu.SemaphoreType.DMA
        in_hbm = pl.BlockSpec(memory_space=pltpu.HBM)
        in_vmem = pl.BlockSpec(memory_space=pltpu.VMEM)
        half = (nz, 2, 8, lon)
        ga, gb, fac, sval = pl.pallas_call(
            functools.partial(kernel, (nz, ny, lat_rows, lon, lat_total)),
            out_shape=(
                jax.ShapeDtypeStruct(half, F32),
                jax.ShapeDtypeStruct(half, F32),
                jax.ShapeDtypeStruct((8, 128), F32),
                jax.ShapeDtypeStruct((8, 128), F32),
            ),
            in_specs=[in_hbm] * 5,
            out_specs=(in_hbm, in_hbm, in_vmem, in_vmem),
            scratch_shapes=[
                vmem((times * lat_rows, lon), BF16),
                vmem((modes, lat_rows, lon), BF16),
                vmem((lat_rows, lon), F32),
                vmem((lat_rows, lon), jnp.int32),
                pltpu.SMEM((modes,), F32),
                vmem(half, F32),
                vmem(half, F32),
                vmem(half, F32),
                vmem(half, F32),
                vmem((nz, 8, lon), F32),
                vmem((8, lon), F32),
                vmem((3, nz - 1, 8, lon), F32),
                vmem((2 * ITERS, 2, 8, 128), F32),
                vmem((2 * ITERS, 2 * ny, 8, 128), F32),
                vmem((ITERS, modes, 8, 128), F32),
                vmem((2, 2, lon), F32),
                vmem((2, 2, lon), F32),
                vmem((2, 2, lon), F32),
                vmem((2, 2, lon), F32),
                vmem((32, width), F32),
                vmem((32, width), F32),
                vmem((32, 128), F32),
                vmem((32, 128), F32),
                vmem((8, 128), F32),
                vmem((8, 128), F32),
                vmem((8, 128), F32),
                dma((5,)),
                dma((3, nz - 1)),
                dma((3, nz - 1)),
                dma((nz + 1,)),
                dma((nz + 1,)),
                dma((3, nz - 1)),
                dma((3, nz - 1)),
                dma((nz + 1,)),
                dma((nz + 1,)),
                dma((2 * ITERS,)),
                dma((2 * ITERS,)),
                dma((2 * ITERS, 2 * ny - 1)),
                dma((2 * ITERS, 2 * ny - 1)),
                dma((ITERS, modes - 1)),
                dma((ITERS, modes - 1)),
                dma((2,)),
                dma((2,)),
                dma((2,)),
                dma((2,)),
            ],
            compiler_params=pltpu.CompilerParams(
                collective_id=0, has_side_effects=True, vmem_limit_bytes=60 * 1024 * 1024
            ),
        )(anomalies.reshape(times * lat_rows, lon), initial, diffusivity, land_mask, threshold)
        small = pl.BlockSpec((8, 128), lambda i: (0, 0))
        block = pl.BlockSpec((2, 2, 8, lon), lambda i: (i, 0, 0, 0))
        current, scores = pl.pallas_call(
            functools.partial(finish, nz),
            grid=(nz // 2,),
            out_shape=(
                jax.ShapeDtypeStruct((2, nz, lat_rows, lon), F32),
                jax.ShapeDtypeStruct((modes, times), F32),
            ),
            in_specs=[block, block, small, small],
            out_specs=(
                pl.BlockSpec((2, 2, lat_rows, lon), lambda i: (0, i, 0, 0)),
                pl.BlockSpec((modes, times), lambda i: (0, 0)),
            ),
        )(ga, gb, fac, sval)
        return current.reshape(modes, lat_rows, lon), scores.T

    return jax.shard_map(
        local,
        mesh=mesh,
        in_specs=(
            P("tm", "tile", None),
            P(None, "tile", None),
            P("tile", None),
            P("tile", None),
            P(),
        ),
        out_specs=(P(None, "tile", None), P("tm", None)),
        check_vma=False,
    )
```

```python
import functools
import math

import jax
import jax.numpy as jnp
from jax import lax
from jax.experimental import pallas as pl
from jax.experimental.pallas import tpu as pltpu
from jax.sharding import PartitionSpec as P

ITERS = 2
EPS = 1e-06
SHRINK = 0.2
MESH = pl.DeviceIdType.MESH
F32 = jnp.float32
BF16 = jnp.bfloat16


def iota(shape, dim):
    return lax.broadcasted_iota(jnp.int32, shape, dim)


def kernel(
    geo,
    anom_hbm,
    init_hbm,
    diff_hbm,
    land_hbm,
    thr_hbm,
    ga_out,
    gb_out,
    fac_out,
    score_out,
    anom,
    init,
    diff,
    land,
    thr_ref,
    pa,
    pb,
    ga,
    gb,
    xb,
    xa,
    zr,
    s1,
    s2,
    q1,
    q2,
    fr,
    hs,
    hr,
    ds,
    dr,
    field,
    dcoef,
    ncoef,
    scoef,
    sval,
    fac,
    msg,
    load_sem,
    z_s,
    z_r,
    x_s,
    x_r,
    g_s,
    g_r,
    y_s,
    y_r,
    a1_s,
    a1_r,
    a2_s,
    a2_r,
    f_s,
    f_r,
    h_s,
    h_r,
    d_s,
    d_r,
):
    nz, ny, lat_rows, lon, lat_total = geo
    cells = lat_total * lon
    ntile = ny * 4
    tm = lax.axis_index("tm")
    tile = lax.axis_index("tile")
    u = lax.div(tm, nz)
    z = lax.rem(tm, nz)
    v = 1 - u
    core = lax.rem(tile, 2)
    xh = lax.rem(lax.div(tile, 2), 2)
    y = lax.div(tile, 4)
    sg = 1 - 2 * core

    def zat(steps):
        return lax.rem(z + steps * sg + 2 * nz, nz)

    plus = {"tm": u * nz + zat(1)}
    plus2 = {"tm": u * nz + zat(2)}
    minus = {"tm": u * nz + zat(-1)}
    across = {"tm": v * nz + z}
    plus_across = {"tm": v * nz + zat(1)}
    minus_across = {"tm": v * nz + zat(-1)}
    below = {"tile": lax.rem(tile + ntile - 1, ntile)}
    above = {"tile": lax.rem(tile + 1, ntile)}
    mate = {"tile": tile + sg}
    spread_to = []
    for dy in sorted(range(ny), key=lambda d: -min(d, ny - d)):
        for dx in (1, 0):
            if dy or dx:
                ox = lax.rem(xh + dx, 2)
                to = lax.rem(y + dy, ny)
                frm = lax.rem(y + ny - dy, ny)
                spread_to.append((frm * 2 + ox, {"tile": to * 4 + ox * 2 + core}))
    factor_to = []
    for dz in sorted(range(nz), key=lambda d: -min(d, nz - d)):
        for du in (1, 0):
            if dz or du:
                ou = lax.rem(u + du, 2)
                to = lax.rem(z + dz, nz)
                frm = lax.rem(z + nz - dz, nz)
                factor_to.append((ou * nz + frm, {"tm": ou * nz + to}))

    loads = [
        pltpu.make_async_copy(init_hbm, init, load_sem.at[0]),
        pltpu.make_async_copy(anom_hbm, anom, load_sem.at[1]),
        pltpu.make_async_copy(diff_hbm, diff, load_sem.at[2]),
        pltpu.make_async_copy(land_hbm, land, load_sem.at[3]),
        pltpu.make_async_copy(thr_hbm, thr_ref, load_sem.at[4]),
    ]
    for copy in loads:
        copy.start()

    barrier = pltpu.get_barrier_semaphore()
    peers = [below, above, mate] + [d for _, d in spread_to] + [d for _, d in factor_to]
    for peer in peers:
        pl.semaphore_signal(barrier, inc=1, device_id=peer, device_id_type=MESH)

    def remote(src, dst, send, recv, where):
        return pltpu.make_async_remote_copy(
            src_ref=src, dst_ref=dst, send_sem=send, recv_sem=recv, device_id=where, device_id_type=MESH
        )

    modes = 2 * nz
    rows = modes * 8
    c_col = iota((rows, 128), 0)
    lane = iota((rows, 128), 1)
    mode_of = lax.rem(lax.div(c_col, 8), 2) * nz + lax.div(c_col, 16)

    def row_in_band(i):
        return jnp.where(i < 4, i, i + 8), i + 4

    loads[0].wait()
    for m in range(modes):
        wide = init[m].astype(F32)
        ga[m % nz, m // nz] = jnp.concatenate([wide[0:4], wide[12:16]], axis=0)
        gb[m % nz, m // nz] = wide[4:12]
    loads[1].wait()

    def square_row():
        a = ga[...].reshape(rows, lon)
        b = gb[...].reshape(rows, lon)
        total = jnp.sum(a * a + b * b, axis=1, keepdims=True)
        spread = jnp.where((lane >= 64) & (lax.rem(lane, 16) == mode_of), total, 0.0)
        return jnp.sum(spread, axis=0, keepdims=True)

    def partial_scores():
        half_a = ga[...].reshape(rows, lon)
        half_b = gb[...].reshape(rows, lon)
        rounded = jnp.concatenate([half_a, half_b], axis=0).astype(BF16)
        product = lax.dot_general(anom[...], rounded, (((1,), (1,)), ((), ())), preferred_element_type=F32)
        times = anom.shape[0] // 16
        prod_a = product[:, :rows].reshape(times, 16, rows)
        prod_b = product[:, rows:].reshape(times, 16, rows)
        here = iota((16, rows), 0)
        in_a, in_b = row_in_band(lax.rem(iota((16, rows), 1), 8))
        kept = jnp.where(here == in_a, prod_a, 0.0) + jnp.where(here == in_b, prod_b, 0.0)
        by_row = jnp.sum(kept, axis=1)
        message = jnp.zeros((8, 128), F32)
        for b in range(4):
            pick = jnp.where(lane == b * 16 + mode_of, 1.0, 0.0).astype(F32)
            message = message + lax.dot_general(
                by_row[b * 8 : (b + 1) * 8],
                pick,
                (((1,), (0,)), ((), ())),
                precision=lax.Precision.HIGHEST,
                preferred_element_type=F32,
            )
        return message

    msg[...] = partial_scores() + square_row()

    pl.semaphore_wait(barrier, len(peers))
    d_copies = [
        remote(ds.at[0], dr.at[1], d_s.at[0], d_r.at[1], below),
        remote(ds.at[1], dr.at[0], d_s.at[1], d_r.at[0], above),
    ]

    def coefficients():
        loads[2].wait()
        loads[3].wait()
        dcoef[...] = jnp.zeros_like(dcoef)
        diffuse = diff[...] * (1.0 + land[...].astype(F32)) * 0.5
        dcoef[8:24, :lon] = diffuse
        ds[0] = diffuse[0:2]
        ds[1] = diffuse[14:16]
        row_index = (tile * lat_rows + iota((32, 128), 0) - 8).astype(F32)
        centre = jnp.sin(jnp.pi * (row_index + 0.5) / lat_total)
        ncoef[...] = SHRINK * jnp.sin(jnp.pi * (row_index + 1.0) / lat_total) / centre
        scoef[...] = SHRINK * jnp.sin(jnp.pi * row_index / lat_total) / centre
        for copy in d_copies:
            copy.start()
        loads[4].wait()

    def step(it, _):
        late = []

        def go(copy, waits):
            copy.start()
            waits.append(copy)

        def tile_first(one, at, message):
            one[it, core] = message
            go(remote(one.at[it, core], one.at[it, core], a1_s.at[at], a1_r.at[at], mate), late)

        def tile_second(one, two, at):
            other = one.at[it, 1 - core]
            remote(other, other, a1_s.at[at], a1_r.at[at], mate).wait_recv()
            me = y * 2 + xh
            two[it, me] = one[it, 0] + one[it, 1]
            for j, (_, where) in enumerate(spread_to):
                go(remote(two.at[it, me], two.at[it, me], a2_s.at[at, j], a2_r.at[at, j], where), late)

        def tile_total(two, at):
            for j, (slot, where) in enumerate(spread_to):
                remote(two.at[it, slot], two.at[it, slot], a2_s.at[at, j], a2_r.at[at, j], where).wait_recv()
            return jnp.sum(two[it], axis=0)

        tile_first(s1, it, msg[...])
        tile_second(s1, s2, it)
        pl.when(it == 0)(coefficients)
        total = tile_total(s2, it)

        @pl.when(it == 0)
        def _():
            fac[...] = lax.rsqrt(pltpu.roll(total, 64, 1) / cells + EPS)

        scores = total * fac[...] / math.sqrt(cells)
        scores = jnp.where(iota((8, 128), 1) < 64, scores, 0.0)
        sval[...] = scores

        tall = jnp.broadcast_to(scores.reshape(8, 1, 128), (8, 16, 128)).reshape(128, 128)
        tall = tall.T.astype(BF16)
        left_a = []
        left_b = []
        for b in range(4):
            pick = jnp.where(lane == b * 16 + mode_of, 1.0, 0.0).astype(BF16)
            wide = jnp.dot(pick, tall, preferred_element_type=F32)
            in_a, in_b = row_in_band(lax.rem(c_col, 8))
            here = lax.rem(lane, 16)
            left_a.append(jnp.where(here == in_a, wide, 0.0).astype(BF16))
            left_b.append(jnp.where(here == in_b, wide, 0.0).astype(BF16))

        def loadings(left):
            part = jnp.dot(jnp.concatenate(left, axis=1), anom[...], preferred_element_type=F32)
            return part.reshape(nz, 2, 8, lon)

        early = []
        offsets = (4, 3, -3, 2, -2, 1, -1, 0)
        place = {off: q for q, off in enumerate(offsets)}
        x_in = [remote(pb.at[zat(off), v], xb.at[q], x_s.at[q], x_r.at[q], across) for q, off in enumerate(offsets)]
        slots = {4: 0, 3: 1, 2: 2, 1: 3, -3: 4, -2: 5, -1: 6}

        def own(c, off):
            if c == 0:
                return pa.at[zat(off), v]
            if c == 1:
                return pa.at[zat(off), u]
            return xb.at[place[off]]

        def prepare(c, off):
            if c == 2:
                q = place[off]
                x_in[q].wait_recv()
                xb[q] = xb[q] + pb[zat(off), u]

        def z_copy(c, off):
            slot = slots[off]
            if off in (4, -3) or (c == 2 and off == 3):
                src = own(c, off)
            elif off == 2:
                src = zr.at[c, 0 if c == 2 else 1]
            else:
                src = zr.at[c, {3: 0, 1: 2, -2: 4, -1: 5}[off]]
            where = plus if off > 0 else minus
            if c == 2 and off == 4:
                where = plus2
            if c == 0 and off in (1, -1):
                where = plus_across if off > 0 else minus_across
            return remote(src, zr.at[c, slot], z_s.at[c, slot], z_r.at[c, slot], where)

        def onward(c, arrived, off):
            prepare(c, off)
            slot = slots[arrived]
            z_copy(c, arrived).wait_recv()
            zr[c, slot] = zr[c, slot] + own(c, off)[...]
            go(z_copy(c, off), early)

        pb[...] = loadings(left_b)
        for copy in x_in[:3]:
            go(copy, late)
        pa[...] = loadings(left_a)
        for off in (4, -3):
            for c in (0, 1):
                go(z_copy(c, off), early)
        x_own = remote(pa.at[z, v], xa, x_s.at[nz], x_r.at[nz], across)
        for copy in x_in[3:] + [x_own]:
            go(copy, late)
        for c in (0, 1):
            onward(c, 4, 3)
            onward(c, -3, -2)
        for off in (4, 3, -3):
            prepare(2, off)
            go(z_copy(2, off), early)
        for c in (0, 1):
            onward(c, 3, 2)
            onward(c, -2, -1)
        prepare(2, 2)
        z_copy(2, 3).wait_recv()
        z_copy(2, 4).wait_recv()
        zr[2, 0] = zr[2, 0] + zr[2, 1] + own(2, 2)[...]
        go(z_copy(2, 2), early)
        onward(2, -3, -2)
        for c in (0, 1):
            onward(c, 2, 1)
        onward(2, 2, 1)
        onward(2, -2, -1)

        def last(c):
            z_copy(c, 1).wait_recv()
            z_copy(c, -1).wait_recv()
            return zr[c, 3] + zr[c, 6]

        x_own.wait_recv()
        sum_a = (pa[z, u] + xa[...]) + last(0) + last(1)
        hs[0] = sum_a[0:2]
        hs[1] = sum_a[6:8]
        h_up = remote(hs.at[1], hr.at[0], h_s.at[1], h_r.at[0], above)
        h_down = remote(hs.at[0], hr.at[1], h_s.at[0], h_r.at[1], below)
        go(h_up, late)
        go(h_down, late)
        prepare(2, 0)
        sum_b = xb[place[0]] + last(2)

        width = field.shape[1]
        col = iota((32, width), 1)

        def wrapped(values):
            right = pltpu.roll(values, lon, 1)
            left = pltpu.roll(values, width - lon, 1)
            return jnp.where(col < lon, values, jnp.where(col < (lon + width) // 2, right, left))

        @pl.when(it == 0)
        def _():
            for copy in d_copies:
                copy.wait_recv()
            dcoef[6:8, :lon] = dr[0]
            dcoef[24:26, :lon] = dr[1]
            dcoef[...] = wrapped(dcoef[...])

        field[8:12, :lon] = sum_a[0:4]
        field[20:24, :lon] = sum_a[4:8]
        field[12:20, :lon] = sum_b
        for copy in early:
            copy.wait_send()
        h_up.wait_recv()
        h_down.wait_recv()
        field[6:8, :lon] = hr[0]
        field[24:26, :lon] = hr[1]
        local_row = iota((32, width), 0) - 8
        global_row = local_row + tile * lat_rows
        inside = (global_row >= 0) & (global_row < lat_total) & (local_row >= -2) & (local_row < 18)
        f = jnp.where(inside, wrapped(field[...]), 0.0)
        north = ncoef[:, 0:1]
        south = scoef[:, 0:1]
        for _pass in range(2):
            east = pltpu.roll(f, width - 1, 1)
            west = pltpu.roll(f, 1, 1)
            upper = pltpu.roll(f, 31, 0)
            lower = pltpu.roll(f, 1, 0)
            change = SHRINK * (east + west - 2.0 * f) + north * (upper - f) + south * (lower - f)
            f = jnp.where(inside, f + dcoef[...] * change, 0.0)
        smoothed = f[8:24, :lon]
        shrunk = jnp.maximum(jnp.abs(smoothed) - thr_ref[tm], 0.0)
        pruned = jnp.where(smoothed < 0.0, -shrunk, shrunk)
        ga[z, u] = jnp.concatenate([pruned[0:4], pruned[12:16]], axis=0)
        gb[z, u] = pruned[4:12]

        def g_ref(c, off):
            if c == 0:
                return ga.at[zat(off), u]
            if c == 1:
                return gb.at[zat(off), u]
            return ga.at[zat(off), v]

        def g_copy(c, off):
            from_here = {1: 0, 2: -1, 3: -2, 4: -3, -1: 0, -2: 1, -3: 2}[off]
            where = plus if off > 0 else minus
            if c == 1 and off == 2:
                from_here = 0
                where = plus2
            ref = g_ref(c, from_here)
            if c == 2 and off in (1, -1):
                ref = ga.at[z, u]
                where = plus_across if off > 0 else minus_across
            return remote(ref, ref, g_s.at[c, slots_g[off]], g_r.at[c, slots_g[off]], where)

        def g_wait(c, off):
            ref = g_ref(c, -off)
            remote(ref, ref, g_s.at[c, slots_g[off]], g_r.at[c, slots_g[off]], plus).wait_recv()

        slots_g = {1: 0, 2: 1, 3: 2, 4: 3, -1: 4, -2: 5, -3: 6}
        queue = []

        def y_send(off):
            ref = gb.at[zat(off), u]
            q = len(queue)
            queue.append(off)
            go(remote(ref, ref, y_s.at[q], y_r.at[q], across), late)

        def pass_on(c, arrived, off):
            g_wait(c, arrived)
            go(g_copy(c, off), late)

        for off in (2, -1, 1):
            go(g_copy(1, off), late)
        for off in (1, -1):
            for c in (0, 2):
                go(g_copy(c, off), late)
        y_send(0)
        a_mine = ga.at[z, u]
        go(remote(a_mine, a_mine, y_s.at[nz], y_r.at[nz], across), late)
        squares = jnp.sum(jnp.sum(pruned * pruned, axis=1, keepdims=True), axis=0, keepdims=True)
        tile_first(q1, ITERS + it, jnp.broadcast_to(squares, (1, 128)))
        tile_second(q1, q2, ITERS + it)
        pass_on(1, 2, 3)
        pass_on(1, -1, -2)
        g_wait(1, 1)
        for off in (-2, 1, -1):
            y_send(off)
        for c in (0, 2):
            pass_on(c, 1, 2)
            pass_on(c, -1, -2)
        here = tile_total(q2, ITERS + it)
        fr[it, tm] = lax.rsqrt(here / cells + EPS)
        for j, (_, where) in enumerate(factor_to):
            go(remote(fr.at[it, tm], fr.at[it, tm], f_s.at[it, j], f_r.at[it, j], where), late)
        pass_on(1, 3, 4)
        pass_on(1, -2, -3)
        for off in (-3, 2):
            y_send(off)
        for c in (0, 2):
            pass_on(c, 2, 3)
            pass_on(c, -2, -3)
        g_wait(1, 4)
        g_wait(1, -3)
        for off in (-4, 3):
            y_send(off)
        for c in (0, 2):
            pass_on(c, 3, 4)
            g_wait(c, -3)
        for c in (0, 2):
            g_wait(c, 4)
        a_other = ga.at[z, v]
        remote(a_other, a_other, y_s.at[nz], y_r.at[nz], across).wait_recv()
        for j, (slot, where) in enumerate(factor_to):
            remote(fr.at[it, slot], fr.at[it, slot], f_s.at[it, j], f_r.at[it, j], where).wait_recv()
        every = fr[it][:, 0, :]
        every = jnp.where(lax.rem(iota((modes, 128), 1), 16) == iota((modes, 128), 0), every, 0.0)
        fac[...] = jnp.broadcast_to(jnp.sum(every, axis=0, keepdims=True), (8, 128))
        for q, off in enumerate(queue):
            ref = gb.at[zat(off), v]
            remote(ref, ref, y_s.at[q], y_r.at[q], across).wait_recv()

        @pl.when(it + 1 < ITERS)
        def _():
            msg[...] = partial_scores()

        for copy in late:
            copy.wait_send()
        return 0

    lax.fori_loop(0, ITERS, step, 0)

    stores = [
        pltpu.make_async_copy(ga, ga_out, load_sem.at[0]),
        pltpu.make_async_copy(gb, gb_out, load_sem.at[1]),
    ]
    for copy in stores:
        copy.start()
    fac_out[...] = fac[...]
    score_out[...] = sval[...]
    for copy in d_copies:
        copy.wait_send()
    for copy in stores:
        copy.wait()


def finish(nz, ga, gb, fac, sval, cur_out, score_out):
    each = ga.shape[0]
    at = pl.program_id(0) * each
    lane = iota((1, 128), 1)
    for b in range(each):
        for u in range(2):
            factor = jnp.sum(jnp.where(lane == u * nz + at + b, fac[0:1], 0.0), axis=1, keepdims=True)
            half_a = ga[b, u] * factor
            cur_out[u, b, 0:4] = half_a[0:4]
            cur_out[u, b, 4:12] = gb[b, u] * factor
            cur_out[u, b, 12:16] = half_a[4:8]
    turned = sval[...].T
    for b in range(4):
        score_out[:, b * 8 : (b + 1) * 8] = turned[b * 16 : (b + 1) * 16]


def solution(mesh):
    nz = mesh.shape["tm"] // 2
    ny = mesh.shape["tile"] // 4

    def local(anomalies, initial, diffusivity, land_mask, threshold):
        times, lat_rows, lon = anomalies.shape
        modes = initial.shape[0]
        lat_total = lat_rows * mesh.shape["tile"]
        width = (lon + 127) // 128 * 128
        vmem = pltpu.VMEM
        dma = pltpu.SemaphoreType.DMA
        in_hbm = pl.BlockSpec(memory_space=pltpu.HBM)
        in_vmem = pl.BlockSpec(memory_space=pltpu.VMEM)
        half = (nz, 2, 8, lon)
        ga, gb, fac, sval = pl.pallas_call(
            functools.partial(kernel, (nz, ny, lat_rows, lon, lat_total)),
            out_shape=(
                jax.ShapeDtypeStruct(half, F32),
                jax.ShapeDtypeStruct(half, F32),
                jax.ShapeDtypeStruct((8, 128), F32),
                jax.ShapeDtypeStruct((8, 128), F32),
            ),
            in_specs=[in_hbm] * 5,
            out_specs=(in_hbm, in_hbm, in_vmem, in_vmem),
            scratch_shapes=[
                vmem((times * lat_rows, lon), BF16),
                vmem((modes, lat_rows, lon), BF16),
                vmem((lat_rows, lon), F32),
                vmem((lat_rows, lon), jnp.int32),
                pltpu.SMEM((modes,), F32),
                vmem(half, F32),
                vmem(half, F32),
                vmem(half, F32),
                vmem(half, F32),
                vmem((nz, 8, lon), F32),
                vmem((8, lon), F32),
                vmem((3, nz - 1, 8, lon), F32),
                vmem((ITERS, 2, 8, 128), F32),
                vmem((ITERS, 2 * ny, 8, 128), F32),
                vmem((ITERS, 2, 1, 128), F32),
                vmem((ITERS, 2 * ny, 1, 128), F32),
                vmem((ITERS, modes, 1, 128), F32),
                vmem((2, 2, lon), F32),
                vmem((2, 2, lon), F32),
                vmem((2, 2, lon), F32),
                vmem((2, 2, lon), F32),
                vmem((32, width), F32),
                vmem((32, width), F32),
                vmem((32, 128), F32),
                vmem((32, 128), F32),
                vmem((8, 128), F32),
                vmem((8, 128), F32),
                vmem((8, 128), F32),
                dma((5,)),
                dma((3, nz - 1)),
                dma((3, nz - 1)),
                dma((nz + 1,)),
                dma((nz + 1,)),
                dma((3, nz - 1)),
                dma((3, nz - 1)),
                dma((nz + 1,)),
                dma((nz + 1,)),
                dma((2 * ITERS,)),
                dma((2 * ITERS,)),
                dma((2 * ITERS, 2 * ny - 1)),
                dma((2 * ITERS, 2 * ny - 1)),
                dma((ITERS, modes - 1)),
                dma((ITERS, modes - 1)),
                dma((2,)),
                dma((2,)),
                dma((2,)),
                dma((2,)),
            ],
            compiler_params=pltpu.CompilerParams(
                collective_id=0, has_side_effects=True, vmem_limit_bytes=60 * 1024 * 1024
            ),
        )(anomalies.reshape(times * lat_rows, lon), initial, diffusivity, land_mask, threshold)
        small = pl.BlockSpec((8, 128), lambda i: (0, 0))
        block = pl.BlockSpec((nz // 2, 2, 8, lon), lambda i: (i, 0, 0, 0))
        current, scores = pl.pallas_call(
            functools.partial(finish, nz),
            grid=(2,),
            out_shape=(
                jax.ShapeDtypeStruct((2, nz, lat_rows, lon), F32),
                jax.ShapeDtypeStruct((modes, times), F32),
            ),
            in_specs=[block, block, small, small],
            out_specs=(
                pl.BlockSpec((2, nz // 2, lat_rows, lon), lambda i: (0, i, 0, 0)),
                pl.BlockSpec((modes, times), lambda i: (0, 0)),
            ),
        )(ga, gb, fac, sval)
        return current.reshape(modes, lat_rows, lon), scores.T

    return jax.shard_map(
        local,
        mesh=mesh,
        in_specs=(
            P("tm", "tile", None),
            P(None, "tile", None),
            P("tile", None),
            P("tile", None),
            P(),
        ),
        out_specs=(P(None, "tile", None), P("tm", None)),
        check_vma=False,
    )
```

```python
import functools
import math

import jax
import jax.numpy as jnp
from jax import lax
from jax.experimental import pallas as pl
from jax.experimental.pallas import tpu as pltpu
from jax.sharding import PartitionSpec as P

ITERS = 2
EPS = 1e-06
SHRINK = 0.2
MESH = pl.DeviceIdType.MESH
F32 = jnp.float32
BF16 = jnp.bfloat16


def iota(shape, dim):
    return lax.broadcasted_iota(jnp.int32, shape, dim)


def kernel(
    geo,
    anom_hbm,
    init_hbm,
    diff_hbm,
    land_hbm,
    thr_hbm,
    ga_out,
    gb_out,
    fac_out,
    score_out,
    anom,
    init,
    diff,
    land,
    thr_ref,
    pa,
    pb,
    ga,
    gb,
    xb,
    xa,
    zr,
    s1,
    s2,
    q1,
    q2,
    fr,
    hs,
    hr,
    ds,
    dr,
    field,
    dcoef,
    ncoef,
    scoef,
    sval,
    fac,
    msg,
    load_sem,
    z_s,
    z_r,
    x_s,
    x_r,
    g_s,
    g_r,
    y_s,
    y_r,
    a1_s,
    a1_r,
    a2_s,
    a2_r,
    f_s,
    f_r,
    h_s,
    h_r,
    d_s,
    d_r,
):
    nz, ny, lat_rows, lon, lat_total = geo
    cells = lat_total * lon
    ntile = ny * 4
    middle = (lon + 255) // 256 * 128
    pieces = (pl.ds(0, middle), pl.ds(middle, lon - middle))
    tm = lax.axis_index("tm")
    tile = lax.axis_index("tile")
    u = lax.div(tm, nz)
    z = lax.rem(tm, nz)
    v = 1 - u
    core = lax.rem(tile, 2)
    xh = lax.rem(lax.div(tile, 2), 2)
    y = lax.div(tile, 4)
    sg = 1 - 2 * core

    def zat(steps):
        return lax.rem(z + steps * sg + 2 * nz, nz)

    plus = {"tm": u * nz + zat(1)}
    plus2 = {"tm": u * nz + zat(2)}
    minus = {"tm": u * nz + zat(-1)}
    across = {"tm": v * nz + z}
    plus_across = {"tm": v * nz + zat(1)}
    minus_across = {"tm": v * nz + zat(-1)}
    below = {"tile": lax.rem(tile + ntile - 1, ntile)}
    above = {"tile": lax.rem(tile + 1, ntile)}
    mate = {"tile": tile + sg}
    spread_to = []
    for dy in sorted(range(ny), key=lambda d: -min(d, ny - d)):
        for dx in (1, 0):
            if dy or dx:
                ox = lax.rem(xh + dx, 2)
                to = lax.rem(y + dy, ny)
                frm = lax.rem(y + ny - dy, ny)
                spread_to.append((frm * 2 + ox, {"tile": to * 4 + ox * 2 + core}))
    factor_to = []
    for dz in sorted(range(nz), key=lambda d: -min(d, nz - d)):
        for du in (1, 0):
            if dz or du:
                ou = lax.rem(u + du, 2)
                to = lax.rem(z + dz, nz)
                frm = lax.rem(z + nz - dz, nz)
                factor_to.append((ou * nz + frm, {"tm": ou * nz + to}))

    loads = [
        pltpu.make_async_copy(init_hbm, init, load_sem.at[0]),
        pltpu.make_async_copy(anom_hbm, anom, load_sem.at[1]),
        pltpu.make_async_copy(diff_hbm, diff, load_sem.at[2]),
        pltpu.make_async_copy(land_hbm, land, load_sem.at[3]),
        pltpu.make_async_copy(thr_hbm, thr_ref, load_sem.at[4]),
    ]
    for copy in loads:
        copy.start()

    barrier = pltpu.get_barrier_semaphore()
    peers = [below, above, mate] + [d for _, d in spread_to] + [d for _, d in factor_to]
    for peer in peers:
        pl.semaphore_signal(barrier, inc=1, device_id=peer, device_id_type=MESH)

    def remote(src, dst, send, recv, where):
        return pltpu.make_async_remote_copy(
            src_ref=src, dst_ref=dst, send_sem=send, recv_sem=recv, device_id=where, device_id_type=MESH
        )

    modes = 2 * nz
    rows = modes * 8
    c_col = iota((rows, 128), 0)
    lane = iota((rows, 128), 1)
    mode_of = lax.rem(lax.div(c_col, 8), 2) * nz + lax.div(c_col, 16)

    def row_in_band(i):
        return jnp.where(i < 4, i, i + 8), i + 4

    loads[0].wait()
    for m in range(modes):
        wide = init[m].astype(F32)
        ga[m % nz, m // nz] = jnp.concatenate([wide[0:4], wide[12:16]], axis=0)
        gb[m % nz, m // nz] = wide[4:12]
    loads[1].wait()

    def square_row():
        a = ga[...].reshape(rows, lon)
        b = gb[...].reshape(rows, lon)
        total = jnp.sum(a * a + b * b, axis=1, keepdims=True)
        spread = jnp.where((lane >= 64) & (lax.rem(lane, 16) == mode_of), total, 0.0)
        return jnp.sum(spread, axis=0, keepdims=True)

    def partial_scores():
        half_a = ga[...].reshape(rows, lon)
        half_b = gb[...].reshape(rows, lon)
        rounded = jnp.concatenate([half_a, half_b], axis=0).astype(BF16)
        product = lax.dot_general(anom[...], rounded, (((1,), (1,)), ((), ())), preferred_element_type=F32)
        times = anom.shape[0] // 16
        prod_a = product[:, :rows].reshape(times, 16, rows)
        prod_b = product[:, rows:].reshape(times, 16, rows)
        here = iota((16, rows), 0)
        in_a, in_b = row_in_band(lax.rem(iota((16, rows), 1), 8))
        kept = jnp.where(here == in_a, prod_a, 0.0) + jnp.where(here == in_b, prod_b, 0.0)
        by_row = jnp.sum(kept, axis=1)
        message = jnp.zeros((8, 128), F32)
        for b in range(4):
            pick = jnp.where(lane == b * 16 + mode_of, 1.0, 0.0).astype(F32)
            message = message + lax.dot_general(
                by_row[b * 8 : (b + 1) * 8],
                pick,
                (((1,), (0,)), ((), ())),
                precision=lax.Precision.HIGHEST,
                preferred_element_type=F32,
            )
        return message

    msg[...] = partial_scores() + square_row()

    pl.semaphore_wait(barrier, len(peers))
    d_copies = [
        remote(ds.at[0], dr.at[1], d_s.at[0], d_r.at[1], below),
        remote(ds.at[1], dr.at[0], d_s.at[1], d_r.at[0], above),
    ]

    def coefficients():
        loads[2].wait()
        loads[3].wait()
        dcoef[...] = jnp.zeros_like(dcoef)
        diffuse = diff[...] * (1.0 + land[...].astype(F32)) * 0.5
        dcoef[8:24, :lon] = diffuse
        ds[0] = diffuse[0:2]
        ds[1] = diffuse[14:16]
        row_index = (tile * lat_rows + iota((32, 128), 0) - 8).astype(F32)
        centre = jnp.sin(jnp.pi * (row_index + 0.5) / lat_total)
        ncoef[...] = SHRINK * jnp.sin(jnp.pi * (row_index + 1.0) / lat_total) / centre
        scoef[...] = SHRINK * jnp.sin(jnp.pi * row_index / lat_total) / centre
        for copy in d_copies:
            copy.start()
        loads[4].wait()

    def step(it, _):
        late = []

        def go(copy, waits):
            copy.start()
            waits.append(copy)

        def tile_first(one, at, message):
            one[it, core] = message
            go(remote(one.at[it, core], one.at[it, core], a1_s.at[at], a1_r.at[at], mate), late)

        def tile_second(one, two, at):
            other = one.at[it, 1 - core]
            remote(other, other, a1_s.at[at], a1_r.at[at], mate).wait_recv()
            me = y * 2 + xh
            two[it, me] = one[it, 0] + one[it, 1]
            for j, (_, where) in enumerate(spread_to):
                go(remote(two.at[it, me], two.at[it, me], a2_s.at[at, j], a2_r.at[at, j], where), late)

        def tile_total(two, at):
            for j, (slot, where) in enumerate(spread_to):
                remote(two.at[it, slot], two.at[it, slot], a2_s.at[at, j], a2_r.at[at, j], where).wait_recv()
            return jnp.sum(two[it], axis=0)

        tile_first(s1, it, msg[...])
        tile_second(s1, s2, it)
        pl.when(it == 0)(coefficients)
        total = tile_total(s2, it)

        @pl.when(it == 0)
        def _():
            fac[...] = lax.rsqrt(pltpu.roll(total, 64, 1) / cells + EPS)

        scores = total * fac[...] / math.sqrt(cells)
        scores = jnp.where(iota((8, 128), 1) < 64, scores, 0.0)
        sval[...] = scores

        tall = jnp.broadcast_to(scores.reshape(8, 1, 128), (8, 16, 128)).reshape(128, 128)
        tall = tall.T.astype(BF16)
        left_a = []
        left_b = []
        for b in range(4):
            pick = jnp.where(lane == b * 16 + mode_of, 1.0, 0.0).astype(BF16)
            wide = jnp.dot(pick, tall, preferred_element_type=F32)
            in_a, in_b = row_in_band(lax.rem(c_col, 8))
            here = lax.rem(lane, 16)
            left_a.append(jnp.where(here == in_a, wide, 0.0).astype(BF16))
            left_b.append(jnp.where(here == in_b, wide, 0.0).astype(BF16))

        def loadings(left):
            part = jnp.dot(jnp.concatenate(left, axis=1), anom[...], preferred_element_type=F32)
            return part.reshape(nz, 2, 8, lon)

        early = []
        offsets = (4, 3, -3, 2, -2, 1, -1, 0)
        place = {off: q for q, off in enumerate(offsets)}
        x_in = [remote(pb.at[zat(off), v], xb.at[q], x_s.at[q], x_r.at[q], across) for q, off in enumerate(offsets)]
        slots = {4: 0, 3: 1, 2: 2, 1: 3, -3: 4, -2: 5, -1: 6}

        def own(c, off):
            if c == 0:
                return pa.at[zat(off), v]
            if c == 1:
                return pa.at[zat(off), u]
            return xb.at[place[off]]

        def prepare(c, off):
            if c == 2:
                q = place[off]
                x_in[q].wait_recv()
                xb[q] = xb[q] + pb[zat(off), u]

        def z_copy(c, off, p):
            slot = slots[off]
            if off in (4, -3) or (c == 2 and off == 3):
                src = own(c, off)
            elif off == 2:
                src = zr.at[c, 0 if c == 2 else 1]
            else:
                src = zr.at[c, {3: 0, 1: 2, -2: 4, -1: 5}[off]]
            where = plus if off > 0 else minus
            if c == 2 and off == 4:
                where = plus2
            if c == 0 and off in (1, -1):
                where = plus_across if off > 0 else minus_across
            src = src.at[:, pieces[p]]
            return remote(src, zr.at[c, slot, :, pieces[p]], z_s.at[c, p, slot], z_r.at[c, p, slot], where)

        def start(c, off):
            prepare(c, off)
            for p in (0, 1):
                go(z_copy(c, off, p), early)

        def onward(c, arrived, off):
            prepare(c, off)
            slot = slots[arrived]
            for p in (0, 1):
                z_copy(c, arrived, p).wait_recv()
                cols = pieces[p]
                zr[c, slot, :, cols] = zr[c, slot, :, cols] + own(c, off)[:, cols]
                go(z_copy(c, off, p), early)

        pb[...] = loadings(left_b)
        for copy in x_in[:3]:
            go(copy, late)
        pa[...] = loadings(left_a)
        for off in (4, -3):
            for c in (0, 1):
                start(c, off)
        x_own = remote(pa.at[z, v], xa, x_s.at[nz], x_r.at[nz], across)
        for copy in x_in[3:] + [x_own]:
            go(copy, late)
        for c in (0, 1):
            onward(c, 4, 3)
            onward(c, -3, -2)
        for off in (4, 3, -3):
            start(2, off)
        for c in (0, 1):
            onward(c, 3, 2)
            onward(c, -2, -1)
        prepare(2, 2)
        for p in (0, 1):
            cols = pieces[p]
            z_copy(2, 3, p).wait_recv()
            z_copy(2, 4, p).wait_recv()
            zr[2, 0, :, cols] = zr[2, 0, :, cols] + zr[2, 1, :, cols] + own(2, 2)[:, cols]
            go(z_copy(2, 2, p), early)
        onward(2, -3, -2)
        for c in (0, 1):
            onward(c, 2, 1)
        onward(2, 2, 1)
        onward(2, -2, -1)

        def last(c):
            for p in (0, 1):
                z_copy(c, 1, p).wait_recv()
                z_copy(c, -1, p).wait_recv()
            return zr[c, 3] + zr[c, 6]

        x_own.wait_recv()
        sum_a = (pa[z, u] + xa[...]) + last(0) + last(1)
        hs[0] = sum_a[0:2]
        hs[1] = sum_a[6:8]
        h_up = remote(hs.at[1], hr.at[0], h_s.at[1], h_r.at[0], above)
        h_down = remote(hs.at[0], hr.at[1], h_s.at[0], h_r.at[1], below)
        go(h_up, late)
        go(h_down, late)
        prepare(2, 0)
        sum_b = xb[place[0]] + last(2)

        width = field.shape[1]
        col = iota((32, width), 1)

        def wrapped(values):
            right = pltpu.roll(values, lon, 1)
            left = pltpu.roll(values, width - lon, 1)
            return jnp.where(col < lon, values, jnp.where(col < (lon + width) // 2, right, left))

        @pl.when(it == 0)
        def _():
            for copy in d_copies:
                copy.wait_recv()
            dcoef[6:8, :lon] = dr[0]
            dcoef[24:26, :lon] = dr[1]
            dcoef[...] = wrapped(dcoef[...])

        field[8:12, :lon] = sum_a[0:4]
        field[20:24, :lon] = sum_a[4:8]
        field[12:20, :lon] = sum_b
        for copy in early:
            copy.wait_send()
        h_up.wait_recv()
        h_down.wait_recv()
        field[6:8, :lon] = hr[0]
        field[24:26, :lon] = hr[1]
        local_row = iota((32, width), 0) - 8
        global_row = local_row + tile * lat_rows
        inside = (global_row >= 0) & (global_row < lat_total) & (local_row >= -2) & (local_row < 18)
        f = jnp.where(inside, wrapped(field[...]), 0.0)
        north = ncoef[:, 0:1]
        south = scoef[:, 0:1]
        for _pass in range(2):
            east = pltpu.roll(f, width - 1, 1)
            west = pltpu.roll(f, 1, 1)
            upper = pltpu.roll(f, 31, 0)
            lower = pltpu.roll(f, 1, 0)
            change = SHRINK * (east + west - 2.0 * f) + north * (upper - f) + south * (lower - f)
            f = jnp.where(inside, f + dcoef[...] * change, 0.0)
        smoothed = f[8:24, :lon]
        shrunk = jnp.maximum(jnp.abs(smoothed) - thr_ref[tm], 0.0)
        pruned = jnp.where(smoothed < 0.0, -shrunk, shrunk)
        ga[z, u] = jnp.concatenate([pruned[0:4], pruned[12:16]], axis=0)
        gb[z, u] = pruned[4:12]

        def g_ref(c, off):
            if c == 0:
                return ga.at[zat(off), u]
            if c == 1:
                return gb.at[zat(off), u]
            return ga.at[zat(off), v]

        def g_copy(c, off, p):
            from_here = {1: 0, 2: -1, 3: -2, 4: -3, -1: 0, -2: 1, -3: 2}[off]
            where = plus if off > 0 else minus
            if c == 1 and off == 2:
                from_here = 0
                where = plus2
            ref = g_ref(c, from_here)
            if c == 2 and off in (1, -1):
                ref = ga.at[z, u]
                where = plus_across if off > 0 else minus_across
            ref = ref.at[:, pieces[p]]
            return remote(ref, ref, g_s.at[c, p, slots_g[off]], g_r.at[c, p, slots_g[off]], where)

        def g_arrive(c, off, p):
            ref = g_ref(c, -off).at[:, pieces[p]]
            remote(ref, ref, g_s.at[c, p, slots_g[off]], g_r.at[c, p, slots_g[off]], plus).wait_recv()

        def g_wait(c, off):
            for p in (0, 1):
                g_arrive(c, off, p)

        def g_start(c, off):
            for p in (0, 1):
                go(g_copy(c, off, p), late)

        slots_g = {1: 0, 2: 1, 3: 2, 4: 3, -1: 4, -2: 5, -3: 6}
        queue = []

        def y_send(off):
            ref = gb.at[zat(off), u]
            q = len(queue)
            queue.append(off)
            go(remote(ref, ref, y_s.at[q], y_r.at[q], across), late)

        def pass_on(c, arrived, off):
            for p in (0, 1):
                g_arrive(c, arrived, p)
                go(g_copy(c, off, p), late)

        for off in (2, -1, 1):
            g_start(1, off)
        for off in (1, -1):
            for c in (0, 2):
                g_start(c, off)
        y_send(0)
        a_mine = ga.at[z, u]
        go(remote(a_mine, a_mine, y_s.at[nz], y_r.at[nz], across), late)
        squares = jnp.sum(jnp.sum(pruned * pruned, axis=1, keepdims=True), axis=0, keepdims=True)
        tile_first(q1, ITERS + it, jnp.broadcast_to(squares, (1, 128)))
        tile_second(q1, q2, ITERS + it)
        pass_on(1, 2, 3)
        pass_on(1, -1, -2)
        g_wait(1, 1)
        for off in (-2, 1, -1):
            y_send(off)
        for c in (0, 2):
            pass_on(c, 1, 2)
            pass_on(c, -1, -2)
        here = tile_total(q2, ITERS + it)
        fr[it, tm] = lax.rsqrt(here / cells + EPS)
        for j, (_, where) in enumerate(factor_to):
            go(remote(fr.at[it, tm], fr.at[it, tm], f_s.at[it, j], f_r.at[it, j], where), late)
        pass_on(1, 3, 4)
        pass_on(1, -2, -3)
        for off in (-3, 2):
            y_send(off)
        for c in (0, 2):
            pass_on(c, 2, 3)
            pass_on(c, -2, -3)
        g_wait(1, 4)
        g_wait(1, -3)
        for off in (-4, 3):
            y_send(off)
        for c in (0, 2):
            pass_on(c, 3, 4)
            g_wait(c, -3)
        for c in (0, 2):
            g_wait(c, 4)
        a_other = ga.at[z, v]
        remote(a_other, a_other, y_s.at[nz], y_r.at[nz], across).wait_recv()
        for j, (slot, where) in enumerate(factor_to):
            remote(fr.at[it, slot], fr.at[it, slot], f_s.at[it, j], f_r.at[it, j], where).wait_recv()
        every = fr[it][:, 0, :]
        every = jnp.where(lax.rem(iota((modes, 128), 1), 16) == iota((modes, 128), 0), every, 0.0)
        fac[...] = jnp.broadcast_to(jnp.sum(every, axis=0, keepdims=True), (8, 128))
        for q, off in enumerate(queue):
            ref = gb.at[zat(off), v]
            remote(ref, ref, y_s.at[q], y_r.at[q], across).wait_recv()

        @pl.when(it + 1 < ITERS)
        def _():
            msg[...] = partial_scores()

        for copy in late:
            copy.wait_send()
        return 0

    lax.fori_loop(0, ITERS, step, 0)

    stores = [
        pltpu.make_async_copy(ga, ga_out, load_sem.at[0]),
        pltpu.make_async_copy(gb, gb_out, load_sem.at[1]),
    ]
    for copy in stores:
        copy.start()
    fac_out[...] = fac[...]
    score_out[...] = sval[...]
    for copy in d_copies:
        copy.wait_send()
    for copy in stores:
        copy.wait()


def finish(nz, ga, gb, fac, sval, cur_out, score_out):
    each = ga.shape[0]
    at = pl.program_id(0) * each
    lane = iota((1, 128), 1)
    for b in range(each):
        for u in range(2):
            factor = jnp.sum(jnp.where(lane == u * nz + at + b, fac[0:1], 0.0), axis=1, keepdims=True)
            half_a = ga[b, u] * factor
            cur_out[u, b, 0:4] = half_a[0:4]
            cur_out[u, b, 4:12] = gb[b, u] * factor
            cur_out[u, b, 12:16] = half_a[4:8]
    turned = sval[...].T
    for b in range(4):
        score_out[:, b * 8 : (b + 1) * 8] = turned[b * 16 : (b + 1) * 16]


def solution(mesh):
    nz = mesh.shape["tm"] // 2
    ny = mesh.shape["tile"] // 4

    def local(anomalies, initial, diffusivity, land_mask, threshold):
        times, lat_rows, lon = anomalies.shape
        modes = initial.shape[0]
        lat_total = lat_rows * mesh.shape["tile"]
        width = (lon + 127) // 128 * 128
        vmem = pltpu.VMEM
        dma = pltpu.SemaphoreType.DMA
        in_hbm = pl.BlockSpec(memory_space=pltpu.HBM)
        in_vmem = pl.BlockSpec(memory_space=pltpu.VMEM)
        half = (nz, 2, 8, lon)
        ga, gb, fac, sval = pl.pallas_call(
            functools.partial(kernel, (nz, ny, lat_rows, lon, lat_total)),
            out_shape=(
                jax.ShapeDtypeStruct(half, F32),
                jax.ShapeDtypeStruct(half, F32),
                jax.ShapeDtypeStruct((8, 128), F32),
                jax.ShapeDtypeStruct((8, 128), F32),
            ),
            in_specs=[in_hbm] * 5,
            out_specs=(in_hbm, in_hbm, in_vmem, in_vmem),
            scratch_shapes=[
                vmem((times * lat_rows, lon), BF16),
                vmem((modes, lat_rows, lon), BF16),
                vmem((lat_rows, lon), F32),
                vmem((lat_rows, lon), jnp.int32),
                pltpu.SMEM((modes,), F32),
                vmem(half, F32),
                vmem(half, F32),
                vmem(half, F32),
                vmem(half, F32),
                vmem((nz, 8, lon), F32),
                vmem((8, lon), F32),
                vmem((3, nz - 1, 8, lon), F32),
                vmem((ITERS, 2, 8, 128), F32),
                vmem((ITERS, 2 * ny, 8, 128), F32),
                vmem((ITERS, 2, 1, 128), F32),
                vmem((ITERS, 2 * ny, 1, 128), F32),
                vmem((ITERS, modes, 1, 128), F32),
                vmem((2, 2, lon), F32),
                vmem((2, 2, lon), F32),
                vmem((2, 2, lon), F32),
                vmem((2, 2, lon), F32),
                vmem((32, width), F32),
                vmem((32, width), F32),
                vmem((32, 128), F32),
                vmem((32, 128), F32),
                vmem((8, 128), F32),
                vmem((8, 128), F32),
                vmem((8, 128), F32),
                dma((5,)),
                dma((3, 2, nz - 1)),
                dma((3, 2, nz - 1)),
                dma((nz + 1,)),
                dma((nz + 1,)),
                dma((3, 2, nz - 1)),
                dma((3, 2, nz - 1)),
                dma((nz + 1,)),
                dma((nz + 1,)),
                dma((2 * ITERS,)),
                dma((2 * ITERS,)),
                dma((2 * ITERS, 2 * ny - 1)),
                dma((2 * ITERS, 2 * ny - 1)),
                dma((ITERS, modes - 1)),
                dma((ITERS, modes - 1)),
                dma((2,)),
                dma((2,)),
                dma((2,)),
                dma((2,)),
            ],
            compiler_params=pltpu.CompilerParams(
                collective_id=0, has_side_effects=True, vmem_limit_bytes=60 * 1024 * 1024
            ),
        )(anomalies.reshape(times * lat_rows, lon), initial, diffusivity, land_mask, threshold)
        small = pl.BlockSpec((8, 128), lambda i: (0, 0))
        block = pl.BlockSpec((nz // 2, 2, 8, lon), lambda i: (i, 0, 0, 0))
        current, scores = pl.pallas_call(
            functools.partial(finish, nz),
            grid=(2,),
            out_shape=(
                jax.ShapeDtypeStruct((2, nz, lat_rows, lon), F32),
                jax.ShapeDtypeStruct((modes, times), F32),
            ),
            in_specs=[block, block, small, small],
            out_specs=(
                pl.BlockSpec((2, nz // 2, lat_rows, lon), lambda i: (0, i, 0, 0)),
                pl.BlockSpec((modes, times), lambda i: (0, 0)),
            ),
        )(ga, gb, fac, sval)
        return current.reshape(modes, lat_rows, lon), scores.T

    return jax.shard_map(
        local,
        mesh=mesh,
        in_specs=(
            P("tm", "tile", None),
            P(None, "tile", None),
            P("tile", None),
            P("tile", None),
            P(),
        ),
        out_specs=(P(None, "tile", None), P("tm", None)),
        check_vma=False,
    )
```

```python
import functools
import math

import jax
import jax.numpy as jnp
from jax import lax
from jax.experimental import pallas as pl
from jax.experimental.pallas import tpu as pltpu
from jax.sharding import PartitionSpec as P

ITERS = 2
EPS = 1e-06
SHRINK = 0.2
MESH = pl.DeviceIdType.MESH
F32 = jnp.float32
BF16 = jnp.bfloat16


def iota(shape, dim):
    return lax.broadcasted_iota(jnp.int32, shape, dim)


def kernel(
    geo,
    anom_hbm,
    init_hbm,
    diff_hbm,
    land_hbm,
    thr_hbm,
    ga_out,
    gb_out,
    fac_out,
    score_out,
    anom,
    init,
    diff,
    land,
    thr_ref,
    pa,
    pb,
    ga,
    gb,
    xb,
    xa,
    zr,
    s1,
    s2,
    q1,
    q2,
    fr,
    hs,
    hr,
    ds,
    dr,
    field,
    dcoef,
    ncoef,
    scoef,
    sval,
    fac,
    msg,
    load_sem,
    z_s,
    z_r,
    x_s,
    x_r,
    g_s,
    g_r,
    y_s,
    y_r,
    a1_s,
    a1_r,
    a2_s,
    a2_r,
    f_s,
    f_r,
    h_s,
    h_r,
    d_s,
    d_r,
):
    nz, ny, lat_rows, lon, lat_total = geo
    cells = lat_total * lon
    ntile = ny * 4
    middle = (lon + 255) // 256 * 128
    pieces = (pl.ds(0, middle), pl.ds(middle, lon - middle))
    tm = lax.axis_index("tm")
    tile = lax.axis_index("tile")
    u = lax.div(tm, nz)
    z = lax.rem(tm, nz)
    v = 1 - u
    core = lax.rem(tile, 2)
    xh = lax.rem(lax.div(tile, 2), 2)
    y = lax.div(tile, 4)
    sg = 1 - 2 * core

    def zat(steps):
        return lax.rem(z + steps * sg + 2 * nz, nz)

    plus = {"tm": u * nz + zat(1)}
    plus2 = {"tm": u * nz + zat(2)}
    minus = {"tm": u * nz + zat(-1)}
    across = {"tm": v * nz + z}
    plus_across = {"tm": v * nz + zat(1)}
    minus_across = {"tm": v * nz + zat(-1)}
    below = {"tile": lax.rem(tile + ntile - 1, ntile)}
    above = {"tile": lax.rem(tile + 1, ntile)}
    mate = {"tile": tile + sg}
    spread_to = []
    for dy in sorted(range(ny), key=lambda d: -min(d, ny - d)):
        for dx in (1, 0):
            if dy or dx:
                ox = lax.rem(xh + dx, 2)
                to = lax.rem(y + dy, ny)
                frm = lax.rem(y + ny - dy, ny)
                spread_to.append((frm * 2 + ox, {"tile": to * 4 + ox * 2 + core}))
    factor_to = []
    for dz in sorted(range(nz), key=lambda d: -min(d, nz - d)):
        for du in (1, 0):
            if dz or du:
                ou = lax.rem(u + du, 2)
                to = lax.rem(z + dz, nz)
                frm = lax.rem(z + nz - dz, nz)
                factor_to.append((ou * nz + frm, {"tm": ou * nz + to}))

    loads = [
        pltpu.make_async_copy(init_hbm, init, load_sem.at[0]),
        pltpu.make_async_copy(anom_hbm, anom, load_sem.at[1]),
        pltpu.make_async_copy(diff_hbm, diff, load_sem.at[2]),
        pltpu.make_async_copy(land_hbm, land, load_sem.at[3]),
        pltpu.make_async_copy(thr_hbm, thr_ref, load_sem.at[4]),
    ]
    for copy in loads:
        copy.start()

    barrier = pltpu.get_barrier_semaphore()
    peers = [below, above, mate] + [d for _, d in spread_to] + [d for _, d in factor_to]
    for peer in peers:
        pl.semaphore_signal(barrier, inc=1, device_id=peer, device_id_type=MESH)

    def remote(src, dst, send, recv, where):
        return pltpu.make_async_remote_copy(
            src_ref=src, dst_ref=dst, send_sem=send, recv_sem=recv, device_id=where, device_id_type=MESH
        )

    modes = 2 * nz
    rows = modes * 8
    c_col = iota((rows, 128), 0)
    lane = iota((rows, 128), 1)
    mode_of = lax.rem(lax.div(c_col, 8), 2) * nz + lax.div(c_col, 16)

    def row_in_band(i):
        return jnp.where(i < 4, i, i + 8), i + 4

    loads[0].wait()
    for m in range(modes):
        wide = init[m].astype(F32)
        ga[m % nz, m // nz] = jnp.concatenate([wide[0:4], wide[12:16]], axis=0)
        gb[m % nz, m // nz] = wide[4:12]
    loads[1].wait()

    def square_row():
        a = ga[...].reshape(rows, lon)
        b = gb[...].reshape(rows, lon)
        total = jnp.sum(a * a + b * b, axis=1, keepdims=True)
        spread = jnp.where((lane >= 64) & (lax.rem(lane, 16) == mode_of), total, 0.0)
        return jnp.sum(spread, axis=0, keepdims=True)

    def partial_scores():
        half_a = ga[...].reshape(rows, lon)
        half_b = gb[...].reshape(rows, lon)
        rounded = jnp.concatenate([half_a, half_b], axis=0).astype(BF16)
        product = lax.dot_general(anom[...], rounded, (((1,), (1,)), ((), ())), preferred_element_type=F32)
        times = anom.shape[0] // 16
        prod_a = product[:, :rows].reshape(times, 16, rows)
        prod_b = product[:, rows:].reshape(times, 16, rows)
        here = iota((16, rows), 0)
        in_a, in_b = row_in_band(lax.rem(iota((16, rows), 1), 8))
        kept = jnp.where(here == in_a, prod_a, 0.0) + jnp.where(here == in_b, prod_b, 0.0)
        by_row = jnp.sum(kept, axis=1)
        message = jnp.zeros((8, 128), F32)
        for b in range(4):
            pick = jnp.where(lane == b * 16 + mode_of, 1.0, 0.0).astype(F32)
            message = message + lax.dot_general(
                by_row[b * 8 : (b + 1) * 8],
                pick,
                (((1,), (0,)), ((), ())),
                precision=lax.Precision.HIGHEST,
                preferred_element_type=F32,
            )
        return message

    msg[...] = partial_scores() + square_row()

    pl.semaphore_wait(barrier, len(peers))
    d_copies = [
        remote(ds.at[0], dr.at[1], d_s.at[0], d_r.at[1], below),
        remote(ds.at[1], dr.at[0], d_s.at[1], d_r.at[0], above),
    ]

    def coefficients():
        loads[2].wait()
        loads[3].wait()
        dcoef[...] = jnp.zeros_like(dcoef)
        diffuse = diff[...] * (1.0 + land[...].astype(F32)) * 0.5
        dcoef[8:24, :lon] = diffuse
        ds[0] = diffuse[0:2]
        ds[1] = diffuse[14:16]
        row_index = (tile * lat_rows + iota((32, 128), 0) - 8).astype(F32)
        centre = jnp.sin(jnp.pi * (row_index + 0.5) / lat_total)
        ncoef[...] = SHRINK * jnp.sin(jnp.pi * (row_index + 1.0) / lat_total) / centre
        scoef[...] = SHRINK * jnp.sin(jnp.pi * row_index / lat_total) / centre
        for copy in d_copies:
            copy.start()
        loads[4].wait()

    def step(it, _):
        late = []

        def go(copy, waits):
            copy.start()
            waits.append(copy)

        def tile_first(one, at, message):
            one[it, core] = message
            go(remote(one.at[it, core], one.at[it, core], a1_s.at[at], a1_r.at[at], mate), late)

        def tile_second(one, two, at):
            other = one.at[it, 1 - core]
            remote(other, other, a1_s.at[at], a1_r.at[at], mate).wait_recv()
            me = y * 2 + xh
            two[it, me] = one[it, 0] + one[it, 1]
            for j, (_, where) in enumerate(spread_to):
                go(remote(two.at[it, me], two.at[it, me], a2_s.at[at, j], a2_r.at[at, j], where), late)

        def tile_total(two, at):
            for j, (slot, where) in enumerate(spread_to):
                remote(two.at[it, slot], two.at[it, slot], a2_s.at[at, j], a2_r.at[at, j], where).wait_recv()
            return jnp.sum(two[it], axis=0)

        tile_first(s1, it, msg[...])
        tile_second(s1, s2, it)
        pl.when(it == 0)(coefficients)
        total = tile_total(s2, it)

        @pl.when(it == 0)
        def _():
            fac[...] = lax.rsqrt(pltpu.roll(total, 64, 1) / cells + EPS)

        scores = total * fac[...] / math.sqrt(cells)
        scores = jnp.where(iota((8, 128), 1) < 64, scores, 0.0)
        sval[...] = scores

        tall = jnp.broadcast_to(scores.reshape(8, 1, 128), (8, 16, 128)).reshape(128, 128)
        tall = tall.T.astype(BF16)
        left_a = []
        left_b = []
        for b in range(4):
            pick = jnp.where(lane == b * 16 + mode_of, 1.0, 0.0).astype(BF16)
            wide = jnp.dot(pick, tall, preferred_element_type=F32)
            in_a, in_b = row_in_band(lax.rem(c_col, 8))
            here = lax.rem(lane, 16)
            left_a.append(jnp.where(here == in_a, wide, 0.0).astype(BF16))
            left_b.append(jnp.where(here == in_b, wide, 0.0).astype(BF16))

        def loadings(left):
            part = jnp.dot(jnp.concatenate(left, axis=1), anom[...], preferred_element_type=F32)
            return part.reshape(nz, 2, 8, lon)

        early = []
        offsets = (4, 3, -3, 2, -2, 1, -1, 0)
        place = {off: q for q, off in enumerate(offsets)}
        x_in = [remote(pb.at[zat(off), v], xb.at[q], x_s.at[q], x_r.at[q], across) for q, off in enumerate(offsets)]
        slots = {4: 0, 3: 1, 2: 2, 1: 3, -3: 4, -2: 5, -1: 6}

        def own(c, off):
            if c == 0:
                return pa.at[zat(off), v]
            if c == 1:
                return pa.at[zat(off), u]
            return xb.at[place[off]]

        def prepare(c, off):
            if c == 2:
                q = place[off]
                x_in[q].wait_recv()
                xb[q] = xb[q] + pb[zat(off), u]

        def z_copy(c, off, p):
            slot = slots[off]
            if off in (4, -3) or (c == 2 and off == 3):
                src = own(c, off)
            elif off == 2:
                src = zr.at[c, 0 if c == 2 else 1]
            else:
                src = zr.at[c, {3: 0, 1: 2, -2: 4, -1: 5}[off]]
            where = plus if off > 0 else minus
            if c == 2 and off == 4:
                where = plus2
            if c == 0 and off in (1, -1):
                where = plus_across if off > 0 else minus_across
            src = src.at[:, pieces[p]]
            return remote(src, zr.at[c, slot, :, pieces[p]], z_s.at[c, p, slot], z_r.at[c, p, slot], where)

        def start(c, off):
            prepare(c, off)
            for p in (0, 1):
                go(z_copy(c, off, p), early)

        def onward(c, arrived, off):
            prepare(c, off)
            slot = slots[arrived]
            for p in (0, 1):
                z_copy(c, arrived, p).wait_recv()
                cols = pieces[p]
                zr[c, slot, :, cols] = zr[c, slot, :, cols] + own(c, off)[:, cols]
                go(z_copy(c, off, p), early)

        pb[...] = loadings(left_b)
        for copy in x_in[:3]:
            go(copy, late)
        pa[...] = loadings(left_a)
        for off in (4, -3):
            for c in (0, 1):
                start(c, off)
        x_own = remote(pa.at[z, v], xa, x_s.at[nz], x_r.at[nz], across)
        for copy in x_in[3:] + [x_own]:
            go(copy, late)
        for c in (0, 1):
            onward(c, 4, 3)
            onward(c, -3, -2)
        for off in (4, 3, -3):
            start(2, off)
        for c in (0, 1):
            onward(c, 3, 2)
            onward(c, -2, -1)
        prepare(2, 2)
        for p in (0, 1):
            cols = pieces[p]
            z_copy(2, 3, p).wait_recv()
            z_copy(2, 4, p).wait_recv()
            zr[2, 0, :, cols] = zr[2, 0, :, cols] + zr[2, 1, :, cols] + own(2, 2)[:, cols]
            go(z_copy(2, 2, p), early)
        onward(2, -3, -2)
        for c in (0, 1):
            onward(c, 2, 1)
        onward(2, 2, 1)
        onward(2, -2, -1)

        def last(c):
            for p in (0, 1):
                z_copy(c, 1, p).wait_recv()
                z_copy(c, -1, p).wait_recv()
            return zr[c, 3] + zr[c, 6]

        x_own.wait_recv()
        sum_a = (pa[z, u] + xa[...]) + last(0) + last(1)
        hs[0] = sum_a[0:2]
        hs[1] = sum_a[6:8]
        h_up = remote(hs.at[1], hr.at[0], h_s.at[1], h_r.at[0], above)
        h_down = remote(hs.at[0], hr.at[1], h_s.at[0], h_r.at[1], below)
        go(h_up, late)
        go(h_down, late)
        prepare(2, 0)
        sum_b = xb[place[0]] + last(2)

        width = field.shape[1]
        col = iota((32, width), 1)

        def wrapped(values):
            right = pltpu.roll(values, lon, 1)
            left = pltpu.roll(values, width - lon, 1)
            return jnp.where(col < lon, values, jnp.where(col < (lon + width) // 2, right, left))

        @pl.when(it == 0)
        def _():
            for copy in d_copies:
                copy.wait_recv()
            dcoef[6:8, :lon] = dr[0]
            dcoef[24:26, :lon] = dr[1]
            dcoef[...] = wrapped(dcoef[...])

        field[8:12, :lon] = sum_a[0:4]
        field[20:24, :lon] = sum_a[4:8]
        field[12:20, :lon] = sum_b
        for copy in early:
            copy.wait_send()
        h_up.wait_recv()
        h_down.wait_recv()
        field[6:8, :lon] = hr[0]
        field[24:26, :lon] = hr[1]
        local_row = iota((32, width), 0) - 8
        global_row = local_row + tile * lat_rows
        inside = (global_row >= 0) & (global_row < lat_total) & (local_row >= -2) & (local_row < 18)
        f = jnp.where(inside, wrapped(field[...]), 0.0)
        north = ncoef[:, 0:1]
        south = scoef[:, 0:1]
        for _pass in range(2):
            east = pltpu.roll(f, width - 1, 1)
            west = pltpu.roll(f, 1, 1)
            upper = pltpu.roll(f, 31, 0)
            lower = pltpu.roll(f, 1, 0)
            change = SHRINK * (east + west - 2.0 * f) + north * (upper - f) + south * (lower - f)
            f = jnp.where(inside, f + dcoef[...] * change, 0.0)
        smoothed = f[8:24, :lon]
        shrunk = jnp.maximum(jnp.abs(smoothed) - thr_ref[tm], 0.0)
        pruned = jnp.where(smoothed < 0.0, -shrunk, shrunk)
        ga[z, u] = jnp.concatenate([pruned[0:4], pruned[12:16]], axis=0)
        gb[z, u] = pruned[4:12]

        def g_ref(c, off):
            if c == 0:
                return ga.at[zat(off), u]
            if c == 1:
                return gb.at[zat(off), u]
            return ga.at[zat(off), v]

        def g_copy(c, off, p):
            from_here = {1: 0, 2: -1, 3: -2, 4: -3, -1: 0, -2: 1, -3: 2}[off]
            where = plus if off > 0 else minus
            if c == 1 and off == 2:
                from_here = 0
                where = plus2
            ref = g_ref(c, from_here)
            if c == 2 and off in (1, -1):
                ref = ga.at[z, u]
                where = plus_across if off > 0 else minus_across
            ref = ref.at[:, pieces[p]]
            return remote(ref, ref, g_s.at[c, p, slots_g[off]], g_r.at[c, p, slots_g[off]], where)

        def g_arrive(c, off, p):
            ref = g_ref(c, -off).at[:, pieces[p]]
            remote(ref, ref, g_s.at[c, p, slots_g[off]], g_r.at[c, p, slots_g[off]], plus).wait_recv()

        def g_wait(c, off):
            for p in (0, 1):
                g_arrive(c, off, p)

        def g_start(c, off):
            for p in (0, 1):
                go(g_copy(c, off, p), late)

        slots_g = {1: 0, 2: 1, 3: 2, 4: 3, -1: 4, -2: 5, -3: 6}
        queue = []

        def y_send(off):
            ref = gb.at[zat(off), u]
            q = len(queue)
            queue.append(off)
            go(remote(ref, ref, y_s.at[q], y_r.at[q], across), late)

        def pass_on(c, arrived, off):
            for p in (0, 1):
                g_arrive(c, arrived, p)
                go(g_copy(c, off, p), late)

        for off in (2, -1, 1):
            g_start(1, off)
        for off in (1, -1):
            for c in (0, 2):
                g_start(c, off)
        y_send(0)
        a_mine = ga.at[z, u]
        go(remote(a_mine, a_mine, y_s.at[nz], y_r.at[nz], across), late)
        squares = jnp.sum(jnp.sum(pruned * pruned, axis=1, keepdims=True), axis=0, keepdims=True)
        tile_first(q1, ITERS + it, jnp.broadcast_to(squares, (1, 128)))
        tile_second(q1, q2, ITERS + it)
        pass_on(1, 2, 3)
        pass_on(1, -1, -2)
        g_wait(1, 1)
        for off in (-2, 1, -1):
            y_send(off)
        for c in (0, 2):
            pass_on(c, 1, 2)
            pass_on(c, -1, -2)
        pass_on(1, 3, 4)
        pass_on(1, -2, -3)
        for off in (-3, 2):
            y_send(off)
        for c in (0, 2):
            pass_on(c, 2, 3)
            pass_on(c, -2, -3)
        here = tile_total(q2, ITERS + it)
        fr[it, tm] = lax.rsqrt(here / cells + EPS)
        for j, (_, where) in enumerate(factor_to):
            go(remote(fr.at[it, tm], fr.at[it, tm], f_s.at[it, j], f_r.at[it, j], where), late)
        g_wait(1, 4)
        g_wait(1, -3)
        for off in (-4, 3):
            y_send(off)
        for c in (0, 2):
            pass_on(c, 3, 4)
            g_wait(c, -3)
        for c in (0, 2):
            g_wait(c, 4)
        a_other = ga.at[z, v]
        remote(a_other, a_other, y_s.at[nz], y_r.at[nz], across).wait_recv()
        for j, (slot, where) in enumerate(factor_to):
            remote(fr.at[it, slot], fr.at[it, slot], f_s.at[it, j], f_r.at[it, j], where).wait_recv()
        every = fr[it][:, 0, :]
        every = jnp.where(lax.rem(iota((modes, 128), 1), 16) == iota((modes, 128), 0), every, 0.0)
        fac[...] = jnp.broadcast_to(jnp.sum(every, axis=0, keepdims=True), (8, 128))
        for q, off in enumerate(queue):
            ref = gb.at[zat(off), v]
            remote(ref, ref, y_s.at[q], y_r.at[q], across).wait_recv()

        @pl.when(it + 1 < ITERS)
        def _():
            msg[...] = partial_scores()

        for copy in late:
            copy.wait_send()
        return 0

    lax.fori_loop(0, ITERS, step, 0)

    stores = [
        pltpu.make_async_copy(ga, ga_out, load_sem.at[0]),
        pltpu.make_async_copy(gb, gb_out, load_sem.at[1]),
    ]
    for copy in stores:
        copy.start()
    fac_out[...] = fac[...]
    score_out[...] = sval[...]
    for copy in d_copies:
        copy.wait_send()
    for copy in stores:
        copy.wait()


def finish(nz, ga, gb, fac, sval, cur_out, score_out):
    each = ga.shape[0]
    at = pl.program_id(0) * each
    lane = iota((1, 128), 1)
    for b in range(each):
        for u in range(2):
            factor = jnp.sum(jnp.where(lane == u * nz + at + b, fac[0:1], 0.0), axis=1, keepdims=True)
            half_a = ga[b, u] * factor
            cur_out[u, b, 0:4] = half_a[0:4]
            cur_out[u, b, 4:12] = gb[b, u] * factor
            cur_out[u, b, 12:16] = half_a[4:8]
    turned = sval[...].T
    for b in range(4):
        score_out[:, b * 8 : (b + 1) * 8] = turned[b * 16 : (b + 1) * 16]


def solution(mesh):
    nz = mesh.shape["tm"] // 2
    ny = mesh.shape["tile"] // 4

    def local(anomalies, initial, diffusivity, land_mask, threshold):
        times, lat_rows, lon = anomalies.shape
        modes = initial.shape[0]
        lat_total = lat_rows * mesh.shape["tile"]
        width = (lon + 127) // 128 * 128
        vmem = pltpu.VMEM
        dma = pltpu.SemaphoreType.DMA
        in_hbm = pl.BlockSpec(memory_space=pltpu.HBM)
        in_vmem = pl.BlockSpec(memory_space=pltpu.VMEM)
        half = (nz, 2, 8, lon)
        ga, gb, fac, sval = pl.pallas_call(
            functools.partial(kernel, (nz, ny, lat_rows, lon, lat_total)),
            out_shape=(
                jax.ShapeDtypeStruct(half, F32),
                jax.ShapeDtypeStruct(half, F32),
                jax.ShapeDtypeStruct((8, 128), F32),
                jax.ShapeDtypeStruct((8, 128), F32),
            ),
            in_specs=[in_hbm] * 5,
            out_specs=(in_hbm, in_hbm, in_vmem, in_vmem),
            scratch_shapes=[
                vmem((times * lat_rows, lon), BF16),
                vmem((modes, lat_rows, lon), BF16),
                vmem((lat_rows, lon), F32),
                vmem((lat_rows, lon), jnp.int32),
                pltpu.SMEM((modes,), F32),
                vmem(half, F32),
                vmem(half, F32),
                vmem(half, F32),
                vmem(half, F32),
                vmem((nz, 8, lon), F32),
                vmem((8, lon), F32),
                vmem((3, nz - 1, 8, lon), F32),
                vmem((ITERS, 2, 8, 128), F32),
                vmem((ITERS, 2 * ny, 8, 128), F32),
                vmem((ITERS, 2, 1, 128), F32),
                vmem((ITERS, 2 * ny, 1, 128), F32),
                vmem((ITERS, modes, 1, 128), F32),
                vmem((2, 2, lon), F32),
                vmem((2, 2, lon), F32),
                vmem((2, 2, lon), F32),
                vmem((2, 2, lon), F32),
                vmem((32, width), F32),
                vmem((32, width), F32),
                vmem((32, 128), F32),
                vmem((32, 128), F32),
                vmem((8, 128), F32),
                vmem((8, 128), F32),
                vmem((8, 128), F32),
                dma((5,)),
                dma((3, 2, nz - 1)),
                dma((3, 2, nz - 1)),
                dma((nz + 1,)),
                dma((nz + 1,)),
                dma((3, 2, nz - 1)),
                dma((3, 2, nz - 1)),
                dma((nz + 1,)),
                dma((nz + 1,)),
                dma((2 * ITERS,)),
                dma((2 * ITERS,)),
                dma((2 * ITERS, 2 * ny - 1)),
                dma((2 * ITERS, 2 * ny - 1)),
                dma((ITERS, modes - 1)),
                dma((ITERS, modes - 1)),
                dma((2,)),
                dma((2,)),
                dma((2,)),
                dma((2,)),
            ],
            compiler_params=pltpu.CompilerParams(
                collective_id=0, has_side_effects=True, vmem_limit_bytes=60 * 1024 * 1024
            ),
        )(anomalies.reshape(times * lat_rows, lon), initial, diffusivity, land_mask, threshold)
        small = pl.BlockSpec((8, 128), lambda i: (0, 0))
        block = pl.BlockSpec((nz // 2, 2, 8, lon), lambda i: (i, 0, 0, 0))
        current, scores = pl.pallas_call(
            functools.partial(finish, nz),
            grid=(2,),
            out_shape=(
                jax.ShapeDtypeStruct((2, nz, lat_rows, lon), F32),
                jax.ShapeDtypeStruct((modes, times), F32),
            ),
            in_specs=[block, block, small, small],
            out_specs=(
                pl.BlockSpec((2, nz // 2, lat_rows, lon), lambda i: (0, i, 0, 0)),
                pl.BlockSpec((modes, times), lambda i: (0, 0)),
            ),
        )(ga, gb, fac, sval)
        return current.reshape(modes, lat_rows, lon), scores.T

    return jax.shard_map(
        local,
        mesh=mesh,
        in_specs=(
            P("tm", "tile", None),
            P(None, "tile", None),
            P("tile", None),
            P("tile", None),
            P(),
        ),
        out_specs=(P(None, "tile", None), P("tm", None)),
        check_vma=False,
    )
```
